32 devices in a mesh: slab: 16 (over z, y, core), coil: 2 (over x).
Axes of the slice: x: 2, y: 2, z: 4, core: 2. Of those that a mesh axis runs over, the one named last changes fastest.
Arguments:
- image: float32 [2, 128, 128, 256], P(None, 'slab'), may hold values from -6 to 6
- sensitivity: float32 [2, 2, 128, 128, 256], P(None, 'coil', 'slab'), may hold values from -4 to 4
- kspace: float32 [2, 2, 128, 128, 256], P(None, 'coil', None, 'slab'), may hold values from -3 to 3
- sampled: int32 [128, 128], P(None, 'slab'), may hold values 0 or 1
- w_in: bfloat16 [27, 16, 2], replicated, may hold values from -0.875 to 0.875
- w_mid: bfloat16 [27, 16, 16], replicated, may hold values from -0.3125 to 0.3125
- w_out: bfloat16 [27, 2, 16], replicated, may hold values from -0.3125 to 0.3125
Outputs:
- refined: float32 [2, 128, 128, 256], P(None, 'slab', 'coil')
- residual: float32 [2, 2, 128, 128, 256], P(None, 'coil', None, 'slab')
The draws below stay inside these ranges and needn't reach their ends.
All inputs are finite; a program needn't handle non-finite values. No bound on the sum of `sampled` on one device may be relied on, other than what follows from the above.
Results may differ from the reference program's by a relative error of at most 0.0023.
Values may be sent and summed in bfloat16 or wider, within the bound.
No kernel may reach another device: no remote copies, remote signals or barrier semaphores. Data moves between devices by JAX's collectives and lax.ppermute only.
A program may use at most 192 MiB of HBM per device.

```python
import jax
import jax.numpy as jnp
from jax import lax

NX = 256
NY = 128
NZ = 128
FEAT = 16
GRAD_STEPS = 2
COILS = 2


def set_ends(drawn, own_key, smallest, top_value):
    longest = drawn.shape.index(max(drawn.shape))
    spots = []
    for shift in (0, 1):
        where = [jax.random.randint(jax.random.fold_in(own_key, axis), (), 0, length) for axis, length in enumerate(drawn.shape)]
        where[longest] = (where[longest] + shift) % drawn.shape[longest]
        spots.append(tuple(where))
    return drawn.at[spots[0]].set(smallest).at[spots[1]].set(top_value)


def block_scale(own_key, shape, shards, smallest, high):
    def one(position, parts):
        steps = jax.random.uniform(jax.random.fold_in(jax.random.fold_in(own_key, 6), position), (parts,), jnp.float32, smallest / len(shards), high / len(shards))
        return jnp.repeat(jnp.exp(steps), shape[position] // parts).reshape((-1,) + (1,) * (len(shape) - position - 1))

    loudness = one(*shards[0])
    for cut in shards[1:]:
        loudness = loudness * one(*cut)
    return loudness


def gaussian(own_key, dims, width, limit, shards=(), dtype=jnp.bfloat16):
    entries = jax.random.normal(own_key, dims, jnp.float32) * width
    if len(shards) > 0:
        entries = block_scale(own_key, dims, shards, -0.22, 0.18) * entries
    return jnp.clip(entries, min=-limit, max=limit).astype(dtype)


def setup_inputs(seed: int = 0) -> dict:
    seeds = jax.random.split(jax.random.key(seed), 8)
    return {
        "image": gaussian(seeds[0], (2, NZ, NY, NX), 1.0, 6.0, ((1, 16),), jnp.float32),
        "sensitivity": gaussian(seeds[1], (2, COILS, NZ, NY, NX), COILS ** -0.5, 4.0, ((1, 2), (2, 16)), jnp.float32),
        "kspace": gaussian(seeds[2], (2, COILS, NZ, NY, NX), 0.5, 3.0, ((1, 2), (3, 16)), jnp.float32),
        "sampled": set_ends((jax.random.randint(seeds[3], (NZ, NY), 0, 5) < 2).astype(jnp.int32), jax.random.fold_in(seeds[3], 1), 0, 1),
        "w_in": gaussian(seeds[4], (27, FEAT, 2), 54 ** -0.5, 0.875),
        "w_mid": gaussian(seeds[5], (27, FEAT, FEAT), (27 * FEAT) ** -0.5, 0.3125),
        "w_out": gaussian(seeds[6], (27, 2, FEAT), (27 * FEAT) ** -0.5, 0.3125),
    }


step_size = 0.5


def conv_layer(values, weight):
    count_out = weight.shape[1]
    count_in = weight.shape[2]
    kernel = weight.astype(jnp.float32).reshape(3, 3, 3, count_out, count_in).transpose(3, 4, 0, 1, 2)
    result = lax.conv_general_dilated(values.astype(jnp.float32)[None], kernel, (1, 1, 1), ((1, 1), (1, 1), (1, 1)), dimension_numbers=("NCDHW", "OIDHW", "NCDHW"), precision=lax.Precision.HIGHEST)
    return result[0]


def reference(image, sensitivity, kspace, sampled, w_in, w_mid, w_out):
    current = lax.complex(image[0], image[1])
    coil_maps = lax.complex(sensitivity[0], sensitivity[1])
    measured = lax.complex(kspace[0], kspace[1])
    weight = sampled.astype(jnp.float32)[:, :, None]

    def normal(estimate):
        def one_coil(summed, pair):
            coil_map, data = pair
            spectrum = jnp.fft.fftn(coil_map * estimate, norm="ortho")
            misfit = weight * (spectrum - data)
            back = jnp.conj(coil_map) * jnp.fft.ifftn(misfit, norm="ortho")
            return summed + back, misfit
        return lax.scan(one_coil, jnp.zeros_like(estimate), (coil_maps, measured))

    misfit = None
    for repeat in range(GRAD_STEPS):
        gradient, misfit = normal(current)
        current = current - step_size * gradient
    start = jnp.stack([jnp.real(current), jnp.imag(current)])
    hidden = jax.nn.relu(conv_layer(start.astype(jnp.bfloat16), w_in)).astype(jnp.bfloat16)
    hidden = jax.nn.relu(conv_layer(hidden, w_mid)).astype(jnp.bfloat16)
    refined = start + conv_layer(hidden, w_out)
    residual = jnp.stack([jnp.real(misfit), jnp.imag(misfit)])
    return refined, residual
```

```python
import math

import jax
import jax.numpy as jnp
import numpy as np
from jax import lax
from jax.experimental import pallas as pl
from jax.experimental.pallas import tpu as pltpu
from jax.sharding import PartitionSpec as P

AXES = ("slab", "coil")
step_size = 0.5
three_pass = lax.Precision.HIGH
wire = jnp.float16
wire_scale = 2.0**-6
not_sampled = 60000.0
sampled_below = 30000.0


def dft(length):
    index = np.arange(length)
    angles = (index[:, None] * index[None, :] % length) * (2.0 * math.pi / length)
    factor = 1.0 / math.sqrt(length)
    return np.cos(angles) * factor, -np.sin(angles) * factor


def split_constant(value):
    high = jnp.asarray(value, jnp.float32).astype(jnp.bfloat16)
    low = (jnp.asarray(value, jnp.float32) - high.astype(jnp.float32)).astype(jnp.bfloat16)
    return jnp.stack([high, low])


def right_matrix(re, im):
    return np.block([[re, im], [-im, re]])


def left_matrix(re, im):
    return np.block([[re, -im], [im, re]])


def split(value):
    high = value.astype(jnp.bfloat16)
    low = (value - high.astype(jnp.float32)).astype(jnp.bfloat16)
    return high, low


def dot(a, b):
    return jnp.dot(a, b, preferred_element_type=jnp.float32)


def from_right(value, matrix):
    high, low = split(value)
    return dot(high, matrix[0]) + dot(low, matrix[0]) + dot(high, matrix[1])


def from_left(matrix, value):
    high, low = split(value)
    return dot(matrix[0], high) + dot(matrix[0], low) + dot(matrix[1], high)


def gradient_kernel(maps, image, data, y_out, y_back, z_out, z_back, current, residual):
    coils, _, nz, ny = maps.shape[1:]
    forward_y, inverse_y = (y_out[0], y_out[1]), (y_back[0], y_back[1])
    forward_z, inverse_z = (z_out[0], z_out[1]), (z_back[0], z_back[1])
    data_re = jnp.concatenate([data[0, c, 0].astype(jnp.float32).T for c in range(coils)], axis=1)
    data_im = jnp.concatenate([data[0, c, 1].astype(jnp.float32).T for c in range(coils)], axis=1)
    measured = jnp.concatenate([data_re, data_im], axis=0)
    mask_half = jnp.where(data_re < sampled_below, 1.0, 0.0)
    mask = jnp.concatenate([mask_half, mask_half], axis=0)
    cur_re = image[0, 0].astype(jnp.float32)
    cur_im = image[0, 1].astype(jnp.float32)
    misfit = None
    for _ in range(2):
        rows = []
        for c in range(coils):
            map_re = maps[0, c, 0].astype(jnp.float32)
            map_im = maps[0, c, 1].astype(jnp.float32)
            coil_re = map_re * cur_re - map_im * cur_im
            coil_im = map_re * cur_im + map_im * cur_re
            rows.append(jnp.concatenate([coil_re, coil_im], axis=1))
        over_y = from_right(jnp.concatenate(rows, axis=0), forward_y)
        planes = [over_y[c * nz : (c + 1) * nz] for c in range(coils)]
        stacked = jnp.concatenate(
            [
                jnp.concatenate([p[:, :ny] for p in planes], axis=1),
                jnp.concatenate([p[:, ny:] for p in planes], axis=1),
            ],
            axis=0,
        )
        spectrum = from_left(forward_z, stacked)
        misfit = mask * (spectrum - measured)
        over_z = from_left(inverse_z, misfit)
        back = from_right(
            jnp.concatenate(
                [
                    jnp.concatenate(
                        [
                            over_z[:nz, c * ny : (c + 1) * ny],
                            over_z[nz:, c * ny : (c + 1) * ny],
                        ],
                        axis=1,
                    )
                    for c in range(coils)
                ],
                axis=0,
            ),
            inverse_y,
        )
        grad_re = None
        for c in range(coils):
            map_re = maps[0, c, 0].astype(jnp.float32)
            map_im = maps[0, c, 1].astype(jnp.float32)
            back_re = back[c * nz : (c + 1) * nz, :ny]
            back_im = back[c * nz : (c + 1) * nz, ny:]
            part_re = map_re * back_re + map_im * back_im
            part_im = map_re * back_im - map_im * back_re
            grad_re = part_re if grad_re is None else grad_re + part_re
            grad_im = part_im if c == 0 else grad_im + part_im
        cur_re = cur_re - step_size * grad_re
        cur_im = cur_im - step_size * grad_im
    current[0, 0] = cur_re
    current[0, 1] = cur_im
    for c in range(coils):
        for k in range(2):
            plane = misfit[k * nz : (k + 1) * nz, c * ny : (c + 1) * ny]
            residual[0, c, k] = plane.T * wire_scale


def gradient_steps(maps, image, data):
    columns, coils, _, nz, ny = maps.shape
    re_y, im_y = dft(ny)
    re_z, im_z = dft(nz)
    constants = [
        split_constant(right_matrix(re_y, im_y)),
        split_constant(right_matrix(re_y, -im_y)),
        split_constant(left_matrix(re_z, im_z)),
        split_constant(left_matrix(re_z, -im_z)),
    ]

    def column(shape):
        return pl.BlockSpec((1,) + shape[1:], lambda i: (i,) + (0,) * (len(shape) - 1))

    def fixed(shape):
        return pl.BlockSpec(shape, lambda i: (0,) * len(shape))

    return pl.pallas_call(
        gradient_kernel,
        grid=(columns,),
        in_specs=[column(maps.shape), column(image.shape), column(data.shape)]
        + [fixed(c.shape) for c in constants],
        out_specs=[column(image.shape), column(data.shape)],
        out_shape=[
            jax.ShapeDtypeStruct(image.shape, jnp.float32),
            jax.ShapeDtypeStruct(data.shape, jnp.float32),
        ],
        name="gradient_steps",
    )(maps, image, data, *constants)


def rounded(count, unit):
    return -(-count // unit) * unit


def banded(weight, columns_out, rows_in, rows_out):
    count_out, count_in = weight.shape[1:]
    columns_in = columns_out + 2
    select = np.zeros((3, columns_out, columns_in), np.float32)
    for shift in range(3):
        select[shift, np.arange(columns_out), np.arange(columns_out) + shift] = 1.0
    taps = weight.reshape(3, 3, 3, count_out, count_in)
    full = jnp.einsum("zyxoj,xab->yaozbj", taps, jnp.asarray(select, weight.dtype))
    full = full.reshape(3, columns_out * count_out, 3, columns_in * count_in)
    full = jnp.pad(
        full,
        (
            (0, 0),
            (0, rows_out - columns_out * count_out),
            (0, 0),
            (0, rows_in - columns_in * count_in),
        ),
    )
    return full.reshape(3 * rows_out, 3 * rows_in)


def conv_kernel(start, current, w_in, w_mid, w_out, keep_1, keep_2, refined, pad_0, pad_1, pad_2):
    nz, _, ny = start.shape

    def zero_ends(ref):
        empty = jnp.zeros(ref.shape[1:], ref.dtype)
        ref[0] = empty
        ref[nz + 1] = empty

    for ref in (pad_0, pad_1, pad_2):
        zero_ends(ref)
    pad_0[1 : nz + 1] = start[...]

    def layer(source, weight, write):
        rows = source.shape[1]
        rows_out = weight.shape[0] // 3
        lane = lax.broadcasted_iota(jnp.int32, (rows_out, ny), 1)

        def step(i, carry):
            z = 2 * i
            near = source[pl.ds(z, 3)].reshape(3 * rows, ny)
            far = source[pl.ds(z + 1, 3)].reshape(3 * rows, ny)
            out = dot(weight[...], jnp.concatenate([near, far], axis=1))
            for k in range(2):
                part = out[:, k * ny : (k + 1) * ny]
                before = pltpu.roll(part[:rows_out], 1, 1)
                after = pltpu.roll(part[2 * rows_out :], ny - 1, 1)
                total = part[rows_out : 2 * rows_out]
                total = total + jnp.where(lane == 0, 0.0, before)
                total = total + jnp.where(lane == ny - 1, 0.0, after)
                write(z + k, total)
            return carry

        lax.fori_loop(0, nz // 2, step, 0)

    def hidden(target, keep):
        def write(z, total):
            target[z + 1] = (jnp.maximum(total, 0.0) * keep[...]).astype(jnp.bfloat16)

        return write

    def last(z, total):
        refined[z] = current[z] + total

    layer(pad_0, w_in, hidden(pad_1, keep_1))
    layer(pad_1, w_mid, hidden(pad_2, keep_2))
    layer(pad_2, w_out, last)


def denoise(current, w_in, w_mid, w_out, size_x):
    columns, _, nz, ny = current.shape
    feat = w_mid.shape[1]
    devices = size_x // columns
    position = lax.axis_index(AXES)
    start = current.astype(jnp.bfloat16)
    left, right, found, hop = [], [], 0, 1
    while found < 3:
        count = min(columns, 3 - found)
        up = [(i, i + hop) for i in range(devices - hop)]
        down = [(j, i) for i, j in up]
        left.insert(0, lax.ppermute(start[columns - count :], AXES, up))
        right.append(lax.ppermute(start[:count], AXES, down))
        found += count
        hop += 1
    padded = jnp.concatenate(left + [start] + right, axis=0)
    rows_0 = rounded((columns + 6) * 2, 16)
    rows_1 = (columns + 4) * feat
    rows_2 = (columns + 2) * feat
    rows_3 = rounded(columns * 2, 8)

    def to_rows(value, rows):
        value = value.transpose(2, 0, 1, 3).reshape(nz, value.shape[0] * 2, ny)
        return jnp.pad(value, ((0, 0), (0, rows - value.shape[1]), (0, 0)))

    def keep(count, before):
        x = position * columns - before + jnp.arange(count, dtype=jnp.int32)
        inside = jnp.where((x >= 0) & (x < size_x), 1.0, 0.0).astype(jnp.float32)
        return jnp.broadcast_to(jnp.repeat(inside, feat)[:, None], (count * feat, ny))

    refined = pl.pallas_call(
        conv_kernel,
        out_shape=jax.ShapeDtypeStruct((nz, rows_3, ny), jnp.float32),
        scratch_shapes=[
            pltpu.VMEM((nz + 2, rows_0, ny), jnp.bfloat16),
            pltpu.VMEM((nz + 2, rows_1, ny), jnp.bfloat16),
            pltpu.VMEM((nz + 2, rows_2, ny), jnp.bfloat16),
        ],
        name="denoise",
    )(
        to_rows(padded, rows_0),
        to_rows(current, rows_3),
        banded(w_in, columns + 4, rows_0, rows_1),
        banded(w_mid, columns + 2, rows_1, rows_2),
        banded(w_out, columns, rows_2, rows_3),
        keep(columns + 4, 2),
        keep(columns + 2, 1),
    )
    return refined[:, : columns * 2].reshape(nz, columns, 2, ny)


def shards(image, sensitivity, kspace, sampled, w_in, w_mid, w_out):
    slabs, groups = lax.axis_size("slab"), lax.axis_size("coil")
    devices = slabs * groups
    _, local_z, ny, nx = image.shape
    local_coils = sensitivity.shape[1]
    coils = local_coils * groups
    nz, local_ky = kspace.shape[2:4]
    columns = nx // devices
    local_y = ny // groups

    maps = sensitivity.astype(wire).transpose(4, 1, 0, 2, 3)
    maps = lax.all_to_all(maps, AXES, 0, 0, tiled=True)
    maps = maps.reshape(slabs, groups, columns, local_coils, 2, local_z, ny)
    maps = maps.transpose(2, 1, 3, 4, 0, 5, 6).reshape(columns, coils, 2, nz, ny)

    own = image.reshape(2, local_z, ny, slabs, groups, columns)
    own = lax.dynamic_index_in_dim(own, lax.axis_index("coil"), 4, keepdims=False)
    own = own.astype(wire).transpose(3, 4, 0, 1, 2)
    own = lax.all_to_all(own, "slab", 0, 0, tiled=True)
    own = own.transpose(1, 2, 0, 3, 4).reshape(columns, 2, nz, ny)

    re_x, im_x = dft(nx)
    forward_x = jnp.asarray(right_matrix(re_x, im_x).reshape(2, nx, 2, nx), jnp.float32)
    inverse_x = jnp.asarray(right_matrix(re_x, -im_x).reshape(2, nx, 2, nx), jnp.float32)
    data = jnp.einsum("aczyr,arbx->xcbyz", kspace, inverse_x, precision=three_pass)
    data = jnp.where(sampled.T[None, None, None] > 0, data, not_sampled).astype(wire)
    data = lax.all_to_all(data, AXES, 0, 0, tiled=True)
    data = data.reshape(slabs, groups, columns, local_coils, 2, local_ky, nz)
    data = data.transpose(2, 1, 3, 4, 0, 5, 6).reshape(columns, coils, 2, ny, nz)

    f32 = jnp.float32
    current, misfit = gradient_steps(maps.astype(f32), own.astype(f32), data.astype(f32))

    misfit = misfit.astype(wire).reshape(columns, groups, local_coils, 2, slabs, local_ky, nz)
    misfit = misfit.transpose(4, 1, 0, 2, 3, 5, 6)
    misfit = misfit.reshape(devices, columns, local_coils, 2, local_ky, nz)
    misfit = lax.all_to_all(misfit, AXES, 0, 0, tiled=True).astype(f32)
    misfit = misfit.reshape(nx, local_coils, 2, local_ky, nz)
    residual = jnp.einsum("xcayz,axbr->bczyr", misfit, forward_x * (1.0 / wire_scale), precision=three_pass)

    refined = denoise(current, w_in, w_mid, w_out, nx)

    largest = jnp.maximum(jnp.max(jnp.abs(refined)), 1e-30)
    exponent = jnp.ceil(jnp.log2(largest)) - 15.0
    sent = (refined * jnp.exp2(-exponent)).astype(wire)
    sent = sent.reshape(slabs, local_z, columns, 2, groups, local_y)
    sent = sent.transpose(0, 4, 2, 3, 1, 5).reshape(devices, columns, 2 * local_z * local_y)
    tag = jnp.broadcast_to(exponent.astype(wire), (devices, columns, ny))
    sent = jnp.concatenate([sent, tag], axis=2)
    sent = lax.all_to_all(sent, AXES, 0, 0, tiled=True)
    scale = jnp.exp2(sent[:, :, -1].astype(f32)).reshape(nx)
    refined = sent[:, :, :-ny].reshape(nx, 2, local_z, local_y).astype(f32)
    refined = refined.transpose(1, 2, 3, 0) * scale
    return (refined, residual)


def solution(mesh):
    placed = (
        P(None, "slab", None, None),
        P(None, "coil", "slab", None, None),
        P(None, "coil", None, "slab", None),
        P(None, "slab"),
        P(),
        P(),
        P(),
    )
    return jax.shard_map(
        shards,
        mesh=mesh,
        in_specs=placed,
        out_specs=(P(None, "slab", "coil", None), P(None, "coil", None, "slab", None)),
        check_vma=False,
    )
```

```python
import math

import jax
import jax.numpy as jnp
import numpy as np
from jax import lax
from jax.experimental import pallas as pl
from jax.experimental.pallas import tpu as pltpu
from jax.sharding import PartitionSpec as P

AXES = ("coil", "slab")
step_size = 0.5
three_pass = lax.Precision.HIGH
wire = jnp.float16
wire_scale = 2.0**-6
not_sampled = 60000.0
sampled_below = 30000.0
steps_per_octave = 64.0


def dft(length):
    index = np.arange(length)
    angles = (index[:, None] * index[None, :] % length) * (2.0 * math.pi / length)
    factor = 1.0 / math.sqrt(length)
    return np.cos(angles) * factor, -np.sin(angles) * factor


def split_constant(value):
    value = jnp.asarray(value, jnp.float32)
    high = value.astype(jnp.bfloat16)
    return high, (value - high.astype(jnp.float32)).astype(jnp.bfloat16)


def complex_matrix(length):
    re, im = dft(length)
    return np.block([[re, im], [-im, re]])


def split(value):
    high = value.astype(jnp.bfloat16)
    low = (value - high.astype(jnp.float32)).astype(jnp.bfloat16)
    return high, low


def dot(a, b):
    return jnp.dot(a, b, preferred_element_type=jnp.float32)


def from_right(value, matrix):
    high, low = split(value)
    rows = value.shape[0]
    both = dot(jnp.concatenate([high, low], axis=0), matrix[0])
    return both[:rows] + both[rows:] + dot(high, matrix[1])


def from_left(matrix, value):
    high, low = split(value)
    rows = matrix.shape[1]
    both = dot(matrix[...].reshape(2 * rows, matrix.shape[2]), high)
    return both[:rows] + both[rows:] + dot(matrix[0], low)


def gradient_kernel(maps, image, data, y_right, y_back, z_left, z_back, current, start, residual):
    columns, coils, _, nz, ny = maps.shape
    step = pl.program_id(0)
    total = columns * pl.num_programs(0)
    rows = current.shape[0] // nz

    def load(ref, *index):
        return ref[index].astype(jnp.float32)

    def to_spectra(estimates):
        pieces = []
        for x, (cur_re, cur_im) in enumerate(estimates):
            for c in range(coils):
                map_re, map_im = load(maps, x, c, 0), load(maps, x, c, 1)
                coil_re = map_re * cur_re - map_im * cur_im
                coil_im = map_re * cur_im + map_im * cur_re
                pieces.append(jnp.concatenate([coil_re, coil_im], axis=1))
        spectra = []
        for x in range(columns):
            lines = jnp.concatenate(pieces[x * coils : (x + 1) * coils], axis=0)
            over_y = from_right(lines, y_right)
            planes = [over_y[c * nz : (c + 1) * nz] for c in range(coils)]
            upper = jnp.concatenate([p[:, :ny] for p in planes], axis=1)
            lower = jnp.concatenate([p[:, ny:] for p in planes], axis=1)
            spectra.append(from_left(z_left, jnp.concatenate([upper, lower], axis=0)))
        return spectra

    def to_gradient(x, misfit):
        over_z = from_left(z_back, misfit)
        pieces = []
        for c in range(coils):
            lanes = slice(c * ny, (c + 1) * ny)
            pieces.append(jnp.concatenate([over_z[:nz, lanes], over_z[nz:, lanes]], axis=1))
        back = from_right(jnp.concatenate(pieces, axis=0), y_back)
        grad_re = jnp.zeros((nz, ny), jnp.float32)
        grad_im = jnp.zeros((nz, ny), jnp.float32)
        for c in range(coils):
            map_re, map_im = load(maps, x, c, 0), load(maps, x, c, 1)
            back_re = back[c * nz : (c + 1) * nz, :ny]
            back_im = back[c * nz : (c + 1) * nz, ny:]
            grad_re += map_re * back_re + map_im * back_im
            grad_im += map_re * back_im - map_im * back_re
        return grad_re, grad_im

    measured, masks, estimates = [], [], []
    for x in range(columns):
        planes = [[load(data, x, c, k).T for c in range(coils)] for k in range(2)]
        data_re, data_im = (jnp.concatenate(p, axis=1) for p in planes)
        keep = jnp.where(data_re < sampled_below, 1.0, 0.0)
        measured.append(jnp.concatenate([data_re, data_im], axis=0))
        masks.append(jnp.concatenate([keep, keep], axis=0))
        estimates.append((load(image, x, 0), load(image, x, 1)))
    misfits = [None] * columns
    for _ in range(2):
        spectra = to_spectra(estimates)
        misfits = [masks[x] * (spectra[x] - measured[x]) for x in range(columns)]
        gradients = [to_gradient(x, misfits[x]) for x in range(columns)]
        estimates = [
            tuple(e - step_size * g for e, g in zip(estimates[x], gradients[x]))
            for x in range(columns)
        ]
    for x in range(columns):
        for k in range(2):
            row = k * total + step * columns + x
            current[pl.ds(row, nz, stride=rows), :] = estimates[x][k]
            start[x, k] = estimates[x][k].astype(jnp.bfloat16)
        for c in range(coils):
            for k in range(2):
                plane = misfits[x][k * nz : (k + 1) * nz, c * ny : (c + 1) * ny]
                residual[x, c, k] = plane.T * wire_scale


def gradient_steps(maps, image, data, rows):
    columns, coils, _, nz, ny = maps.shape
    right = {n: jnp.stack(split_constant(complex_matrix(n))) for n in {ny, nz}}
    left = {n: jnp.stack(split_constant(complex_matrix(n).T)) for n in {ny, nz}}
    constants = [right[ny], left[ny], left[nz], right[nz]]
    together = math.gcd(columns, 2)

    def column(shape):
        return pl.BlockSpec((together,) + shape[1:], lambda i: (i,) + (0,) * (len(shape) - 1))

    def fixed(shape):
        return pl.BlockSpec(shape, lambda i: (0,) * len(shape))

    return pl.pallas_call(
        gradient_kernel,
        grid=(columns // together,),
        in_specs=[column(maps.shape), column(image.shape), column(data.shape)]
        + [fixed(c.shape) for c in constants],
        out_specs=[fixed((nz * rows, ny)), column(image.shape), column(data.shape)],
        out_shape=[
            jax.ShapeDtypeStruct((nz * rows, ny), jnp.float32),
            jax.ShapeDtypeStruct(image.shape, jnp.bfloat16),
            jax.ShapeDtypeStruct(data.shape, jnp.float32),
        ],
        name="gradient_steps",
    )(maps, image, data, *constants)


def rounded(count, unit):
    return -(-count // unit) * unit


def banded(weight, columns_out, order):
    columns_in = columns_out + 2
    select = np.zeros((3, columns_out, columns_in), np.float32)
    for shift in range(3):
        select[shift, np.arange(columns_out), np.arange(columns_out) + shift] = 1.0
    taps = weight.reshape((3, 3, 3) + weight.shape[1:])
    return jnp.einsum("zyxoj,xab->" + order, taps, jnp.asarray(select, weight.dtype))


def matrices(w_in, w_mid, w_out, columns, block, rows, halo_rows):
    feat = w_mid.shape[1]
    first = banded(w_in, columns + 4, "aozyjb")
    own = first[..., 3 : columns + 3].reshape(-1, 3, 3, 2 * columns)
    own = jnp.pad(own, ((0, 0),) * 3 + ((0, rows - 2 * columns),))
    sides = jnp.concatenate([first[..., :3], first[..., columns + 3 :]], axis=-1)
    sides = jnp.swapaxes(sides, -1, -2).reshape(-1, 3, 3, 12)
    sides = jnp.pad(sides, ((0, 0),) * 3 + ((0, halo_rows - 12),))
    first = jnp.concatenate([own, sides], axis=-1).reshape((columns + 4) * feat, -1)
    middle = banded(w_mid, block, "yaozbj").reshape(3 * block * feat, -1)
    last = banded(w_out, columns, "zyoabj").reshape(9, 2 * columns, -1)
    last = jnp.pad(last, ((0, 0), (0, rows - 2 * columns), (0, 0)))
    return first, middle, last.reshape(9 * rows, -1)


def conv_kernel(place, current, left, right, w_in, w_mid, w_out, packed, pad_0, pad_1, pad_2, halo, refined):
    rows_1, rows_2 = pad_1.shape[1], pad_2.shape[1]
    nz, ny = refined.shape[0], refined.shape[2]
    rows = refined.shape[1]
    halo_rows = halo.shape[0] // nz
    bf16, f32 = jnp.bfloat16, jnp.float32

    for ref in (pad_0, pad_1):
        empty = jnp.zeros(ref.shape[1:], ref.dtype)
        ref[0] = empty
        ref[nz + 1] = empty

    def shifted(value, by):
        lane = lax.broadcasted_iota(jnp.int32, value.shape, 1)
        edge = 0 if by == 1 else ny - 1
        return jnp.where(lane == edge, 0.0, pltpu.roll(value, by % ny, 1))

    def inside(count, before):
        feat = (rows_1 - rows_2) // 2
        row = lax.broadcasted_iota(jnp.int32, (count, ny), 0)
        x = place[0] - before + row // feat
        return jnp.where((x >= 0) & (x < place[1]), 1.0, 0.0)

    keep_1, keep_2 = inside(rows_1, 2), inside(rows_2, 1)

    for side, ref in enumerate((left, right)):
        for column in range(3):
            for k in range(2):
                row = 6 * side + 2 * column + k
                halo[pl.ds(row, nz, stride=halo_rows), :] = ref[column, k].astype(f32)
    for row in range(12, halo_rows):
        halo[pl.ds(row, nz, stride=halo_rows), :] = jnp.zeros((nz, ny), f32)

    def spread(z, carry):
        own = current[pl.ds(pl.multiple_of(z * rows, 8), rows), :]
        sides = halo[pl.ds(pl.multiple_of(z * halo_rows, 8), halo_rows), :]
        value = jnp.concatenate([own, sides], axis=0)
        shifts = [shifted(value, 1), value, shifted(value, -1)]
        pad_0[z + 1] = jnp.concatenate(shifts, axis=0).astype(bf16)
        return carry

    def pair(block):
        near = jnp.concatenate([block[0], block[1], block[2]], axis=0)
        far = jnp.concatenate([block[1], block[2], block[3]], axis=0)
        return jnp.concatenate([near, far], axis=1)

    def first(i):
        out = dot(w_in[...], pair(pad_0[pl.ds(2 * i, 4)]))
        for k in range(2):
            part = jnp.maximum(out[:, k * ny : (k + 1) * ny], 0.0) * keep_1
            pad_1[2 * i + k + 1] = part.astype(bf16)

    block_out = w_mid.shape[0] // 3
    block_in = w_mid.shape[1] // 3

    def middle(i):
        for b in range(rows_2 // block_out):
            low = b * block_out
            out = dot(w_mid[...], pair(pad_1[pl.ds(2 * i, 4), low : low + block_in]))
            for k in range(2):
                part = out[:, k * ny : (k + 1) * ny]
                total = part[block_out : 2 * block_out]
                total = total + shifted(part[:block_out], 1)
                total = total + shifted(part[2 * block_out :], -1)
                total = jnp.maximum(total, 0.0) * keep_2[low : low + block_out]
                pad_2[2 * i + k, low : low + block_out] = total.astype(bf16)

    def finish(z, total, largest):
        out = total[rows : 2 * rows]
        out = out + shifted(total[:rows], 1) + shifted(total[2 * rows :], -1)
        out = out + current[pl.ds(pl.multiple_of(z * rows, 8), rows), :]
        refined[z] = out
        return jnp.maximum(largest, jnp.abs(out))

    def last(i, carry):
        older, newer, largest = carry
        both = jnp.concatenate([pad_2[2 * i], pad_2[2 * i + 1]], axis=1)
        out = dot(w_out[...], both)
        for k in range(2):
            part = out[:, k * ny : (k + 1) * ny]
            z = 2 * i + k - 1
            total = older + part[6 * rows :]
            if k == 0:
                total = jnp.where(i > 0, total, 0.0)
            largest = finish(jnp.maximum(z, 0), total, largest)
            older, newer = newer + part[3 * rows : 6 * rows], part[: 3 * rows]
        return older, newer, largest

    lax.fori_loop(0, nz, spread, 0, unroll=4)

    def alone(step):
        def run(i, carry):
            step(i)
            return carry

        return run

    lax.fori_loop(0, nz // 2, alone(first), 0, unroll=4)
    lax.fori_loop(0, nz // 2, alone(middle), 0, unroll=8)
    sums = jnp.zeros((3 * rows, ny), f32)
    carry = (sums, sums, jnp.zeros((rows, ny), f32))
    older, _, largest = lax.fori_loop(0, nz // 2, last, carry, unroll=4)
    largest = finish(nz - 1, older, largest)

    if packed.dtype != jnp.int16:
        packed[...] = refined[...]
        return

    groups, slabs, sent_rows, _ = packed.shape
    columns = rows // 2
    top = jnp.maximum(jnp.max(largest, axis=(0, 1), keepdims=True), 1e-30)
    code = jnp.ceil(jnp.log(top * (1.0 / 32000.0)) * (steps_per_octave / math.log(2.0)))
    factor = jnp.exp(code * (-math.log(2.0) / steps_per_octave))
    lane = lax.broadcasted_iota(jnp.int32, (columns, ny), 1)
    tag = jnp.broadcast_to(code, (16, ny)).astype(jnp.int32).astype(jnp.int16)
    for c in range(groups):
        for s in range(slabs):
            packed[c, s, sent_rows - 16 :] = tag

    def pack(s, carry):
        for z in range(0, nz // slabs, 2):
            halves = [[], []]
            for k in range(2):
                value = jnp.round(refined[s * (nz // slabs) + z + k] * factor)
                re, im = value[:columns], value[columns:]
                halves[0].append(jnp.where(lane < ny // 2, re, pltpu.roll(im, ny // 2, 1)))
                halves[1].append(jnp.where(lane < ny // 2, pltpu.roll(re, ny // 2, 1), im))
            for c in range(2):
                both = jnp.concatenate(halves[c], axis=0).astype(jnp.int32).astype(jnp.int16)
                packed[c, s, z * columns : (z + 2) * columns] = both
        return carry

    lax.fori_loop(0, slabs, pack, 0)


def denoise(current, left, right, weights, out_shape, size_x):
    w_in, w_mid, w_out = weights
    nz, ny = left.shape[2:]
    columns = size_x // lax.axis_size(AXES)
    rows = current.shape[0] // nz
    halo_rows = w_in.shape[1] // 9 - rows
    place = jnp.stack([lax.axis_index(AXES) * columns, jnp.int32(size_x)])
    flops = nz * ny * sum(2 * m.shape[0] * m.shape[1] for m in weights)
    return pl.pallas_call(
        conv_kernel,
        in_specs=[pl.BlockSpec(memory_space=pltpu.SMEM)]
        + [pl.BlockSpec(memory_space=pltpu.VMEM)] * 6,
        out_specs=pl.BlockSpec(memory_space=pltpu.VMEM),
        out_shape=out_shape,
        scratch_shapes=[
            pltpu.VMEM((nz + 2, w_in.shape[1] // 3, ny), jnp.bfloat16),
            pltpu.VMEM((nz + 2, w_in.shape[0], ny), jnp.bfloat16),
            pltpu.VMEM((nz, w_out.shape[1], ny), jnp.bfloat16),
            pltpu.VMEM((nz * halo_rows, ny), jnp.float32),
            pltpu.VMEM((nz, rows, ny), jnp.float32),
        ],
        cost_estimate=pl.CostEstimate(
            flops=flops, transcendentals=0, bytes_accessed=8 * current.size
        ),
        name="denoise",
    )(place, current, left, right, w_in, w_mid, w_out)


def unpack_kernel(values, tag, out):
    devices, both, lanes = values.shape
    columns = both // 2
    code = tag[:, :1].astype(jnp.int32).astype(jnp.float32)
    factor = jnp.exp(code * (math.log(2.0) / steps_per_octave))
    value = values[...].astype(jnp.int32).astype(jnp.float32) * factor
    for k in range(2):
        plane = value[:, k * columns : (k + 1) * columns].reshape(devices * columns, lanes)
        plane = plane.T
        out[0, k] = plane[: lanes // 2]
        out[1, k] = plane[lanes // 2 :]


def unpack(sent, columns, local_z):
    devices, sent_rows, lanes = sent.shape
    return pl.pallas_call(
        unpack_kernel,
        grid=(local_z // 2,),
        in_specs=[
            pl.BlockSpec((devices, 2 * columns, lanes), lambda i: (0, i, 0)),
            pl.BlockSpec((devices, 16, lanes), lambda i: (0, sent_rows // 16 - 1, 0)),
        ],
        out_specs=pl.BlockSpec((2, 2, lanes // 2, devices * columns), lambda i: (0, i, 0, 0)),
        out_shape=jax.ShapeDtypeStruct(
            (2, local_z, lanes // 2, devices * columns), jnp.float32
        ),
        name="unpack",
    )(sent, sent)


def neighbours(start, slabs, groups):
    devices = slabs * groups
    columns = start.shape[0]
    place = [i % slabs * groups + i // slabs for i in range(devices)]
    left, right, found, hop = [], [], 0, 1
    while found < 3:
        count = min(columns, 3 - found)
        up = [(place[i], place[i + hop]) for i in range(devices - hop)]
        down = [(j, i) for i, j in up]
        left.insert(0, lax.ppermute(start[columns - count :], ("slab", "coil"), up))
        right.append(lax.ppermute(start[:count], ("slab", "coil"), down))
        found += count
        hop += 1
    return jnp.concatenate(left, axis=0), jnp.concatenate(right, axis=0)


def shards(image, sensitivity, kspace, sampled, w_in, w_mid, w_out):
    slabs, groups = lax.axis_size("slab"), lax.axis_size("coil")
    devices = slabs * groups
    _, local_z, ny, nx = image.shape
    local_coils = sensitivity.shape[1]
    coils = local_coils * groups
    nz, local_ky = kspace.shape[2:4]
    columns = nx // devices
    local_y = ny // groups

    rows = rounded(2 * columns, 8)
    halo_rows = rounded(rows + 12, 16) - rows
    block = (columns + 2) // math.gcd(columns + 2, 2)
    weights = matrices(w_in, w_mid, w_out, columns, block, rows, halo_rows)

    transform_x = jnp.asarray(complex_matrix(nx).reshape(2, nx, 2, nx), jnp.float32)
    data = jnp.einsum("aczyr,bxar->xcbyz", kspace, transform_x, precision=three_pass)
    data = jnp.where(sampled.T[None, None, None] > 0, data, not_sampled).astype(wire)
    data = lax.all_to_all(data, AXES, 0, 0, tiled=True)
    data = data.reshape(groups, slabs, columns, local_coils, 2, local_ky, nz)
    data = data.transpose(2, 0, 3, 4, 1, 5, 6).reshape(columns, coils, 2, ny, nz)

    parts = math.gcd(local_z, groups)
    share = local_z // parts
    own = lax.dynamic_slice_in_dim(image, lax.axis_index("coil") % parts * share, share, 1)
    sent = jnp.concatenate([sensitivity.reshape(-1, ny, nx), own.reshape(-1, ny, nx)], axis=0)
    sent = sent.astype(wire).transpose(2, 0, 1)
    sent = lax.all_to_all(sent, AXES, 0, 0, tiled=True)
    sent, weights = lax.optimization_barrier((sent, weights))
    cut = 2 * local_coils * local_z
    maps = sent[:, :cut].reshape(groups, slabs, columns, 2, local_coils, local_z, ny)
    maps = maps.transpose(2, 0, 4, 3, 1, 5, 6).reshape(columns, coils, 2, nz, ny)
    own = sent[:, cut:].reshape(groups, slabs, columns, 2, share, ny)[:parts]
    own = own.transpose(2, 3, 1, 0, 4, 5).reshape(columns, 2, nz, ny)

    f32 = jnp.float32
    current, start, misfit = gradient_steps(
        maps.astype(f32), own.astype(f32), data.astype(f32), rows
    )
    if rows > 2 * columns:
        used = jnp.arange(rows, dtype=jnp.int32)[:, None] < 2 * columns
        current = jnp.where(used, current.reshape(nz, rows, ny), 0.0).reshape(-1, ny)

    received = neighbours(start, slabs, groups)
    misfit = misfit.astype(wire).reshape(columns, groups, local_coils, 2, slabs, local_ky, nz)
    misfit = misfit.transpose(1, 4, 0, 2, 3, 5, 6)
    misfit = misfit.reshape(devices, columns, local_coils, 2, local_ky, nz)
    received, misfit = lax.optimization_barrier((received, misfit))
    misfit = lax.all_to_all(misfit, AXES, 0, 0, tiled=True)

    aligned = columns % 8 == 0 and local_z % 2 == 0 and ny == 128 and groups == 2
    if aligned:
        shape = (groups, slabs, local_z * columns + 16, ny)
        out_shape = jax.ShapeDtypeStruct(shape, jnp.int16)
    else:
        out_shape = jax.ShapeDtypeStruct((nz, rows, ny), f32)
    refined = denoise(current, *received, weights, out_shape, nx)
    refined, misfit = lax.optimization_barrier((refined, misfit))

    misfit = misfit.astype(f32).reshape(nx, local_coils, 2, local_ky, nz) * (1.0 / wire_scale)
    residual = jnp.einsum("xcayz,axbr->bczyr", misfit, transform_x, precision=three_pass)

    if aligned:
        sent = refined.reshape(devices, -1, ny)
        sent = lax.all_to_all(sent, AXES, 0, 0, tiled=True)
        return unpack(sent, columns, local_z), residual
    refined = refined[:, : 2 * columns].reshape(nz, 2, columns, ny)
    largest = jnp.maximum(jnp.max(jnp.abs(refined)), 1e-30)
    exponent = jnp.ceil(jnp.log2(largest)) - 15.0
    sent = (refined * jnp.exp2(-exponent)).astype(wire)
    sent = sent.reshape(slabs, local_z, 2, columns, groups, local_y)
    sent = sent.transpose(4, 0, 3, 2, 1, 5).reshape(devices, columns, 2 * local_z * local_y)
    tag = jnp.broadcast_to(exponent.astype(wire), (devices, columns, ny))
    sent = jnp.concatenate([sent, tag], axis=2)
    sent = lax.all_to_all(sent, AXES, 0, 0, tiled=True)
    scale = jnp.exp2(sent[:, :, -1].astype(f32)).reshape(nx)
    refined = sent[:, :, :-ny].reshape(nx, 2, local_z, local_y).astype(f32)
    refined = refined.transpose(1, 2, 3, 0) * scale
    return (refined, residual)


def solution(mesh):
    placed = (
        P(None, "slab", None, None),
        P(None, "coil", "slab", None, None),
        P(None, "coil", None, "slab", None),
        P(None, "slab"),
        P(),
        P(),
        P(),
    )
    return jax.shard_map(
        shards,
        mesh=mesh,
        in_specs=placed,
        out_specs=(P(None, "slab", "coil", None), P(None, "coil", None, "slab", None)),
        check_vma=False,
    )
```

```python
import functools
import math

import jax
import jax.numpy as jnp
import numpy as np
from jax import lax
from jax.experimental import pallas as pl
from jax.experimental.layout import Layout, with_layout_constraint
from jax.experimental.pallas import tpu as pltpu
from jax.sharding import PartitionSpec as P

AXES = ("coil", "slab")
step_size = 0.5
three_pass = lax.Precision.HIGH
wire = jnp.float16
wire_scale = 2.0**-6
not_sampled = 60000.0
sampled_below = 30000.0
steps_per_octave = 64.0
code_bias = 8192.0


def dft(length):
    index = np.arange(length)
    angles = (index[:, None] * index[None, :] % length) * (2.0 * math.pi / length)
    factor = 1.0 / math.sqrt(length)
    return np.cos(angles) * factor, -np.sin(angles) * factor


def split_constant(value):
    value = jnp.asarray(value, jnp.float32)
    high = value.astype(jnp.bfloat16)
    return high, (value - high.astype(jnp.float32)).astype(jnp.bfloat16)


def complex_matrix(length):
    re, im = dft(length)
    return np.block([[re, im], [-im, re]])


def split(value):
    high = value.astype(jnp.bfloat16)
    low = (value - high.astype(jnp.float32)).astype(jnp.bfloat16)
    return high, low


def dot(a, b):
    return jnp.dot(a, b, preferred_element_type=jnp.float32)


def from_right(value, matrix):
    high, low = split(value)
    rows = value.shape[0]
    both = dot(jnp.concatenate([high, low], axis=0), matrix[0])
    return both[:rows] + both[rows:] + dot(high, matrix[1])


def from_left(matrix, value):
    high, low = split(value)
    rows = matrix.shape[1]
    both = dot(matrix[...].reshape(2 * rows, matrix.shape[2]), high)
    return both[:rows] + both[rows:] + dot(matrix[0], low)


def load(ref, *index):
    return ref[index].astype(jnp.float32)


def load_plane(ref, slabs, *index):
    plane = load(ref, *index)
    block = plane.shape[0] // slabs
    if slabs > 1 and index[1] % 2 == 1:
        parts = [plane[s * block : (s + 1) * block] for s in reversed(range(slabs))]
        plane = jnp.concatenate(parts, axis=0)
    return plane


def to_spectrum(maps, slabs, x, estimate, y_right, z_left):
    coils, _, nz, ny = maps.shape[1:]
    cur_re, cur_im = estimate
    pieces = []
    for c in range(coils):
        map_re, map_im = (load_plane(maps, slabs, x, c, k) for k in range(2))
        coil_re = map_re * cur_re - map_im * cur_im
        coil_im = map_re * cur_im + map_im * cur_re
        pieces.append(jnp.concatenate([coil_re, coil_im], axis=1))
    over_y = from_right(jnp.concatenate(pieces, axis=0), y_right)
    planes = [over_y[c * nz : (c + 1) * nz] for c in range(coils)]
    upper = jnp.concatenate([p[:, :ny] for p in planes], axis=1)
    lower = jnp.concatenate([p[:, ny:] for p in planes], axis=1)
    return from_left(z_left, jnp.concatenate([upper, lower], axis=0))


def to_gradient(maps, slabs, x, misfit, y_back, z_back):
    coils, _, nz, ny = maps.shape[1:]
    over_z = from_left(z_back, misfit)
    pieces = []
    for c in range(coils):
        lanes = slice(c * ny, (c + 1) * ny)
        pieces.append(jnp.concatenate([over_z[:nz, lanes], over_z[nz:, lanes]], axis=1))
    back = from_right(jnp.concatenate(pieces, axis=0), y_back)
    grad_re = jnp.zeros((nz, ny), jnp.float32)
    grad_im = jnp.zeros((nz, ny), jnp.float32)
    for c in range(coils):
        map_re, map_im = (load_plane(maps, slabs, x, c, k) for k in range(2))
        back_re = back[c * nz : (c + 1) * nz, :ny]
        back_im = back[c * nz : (c + 1) * nz, ny:]
        grad_re += map_re * back_re + map_im * back_im
        grad_im += map_re * back_im - map_im * back_re
    return grad_re, grad_im


def spectrum_kernel(slabs, maps, image, y_right, z_left, spectrum):
    for x in range(maps.shape[0]):
        estimate = (load(image, x, 0), load(image, x, 1))
        spectrum[x] = to_spectrum(maps, slabs, x, estimate, y_right, z_left)


def gradient_kernel(slabs, data_slabs, maps, image, first, data, y_right, y_back, z_left, z_back, current, low, high, residual):
    columns, coils, _, nz, ny = maps.shape
    step = pl.program_id(0)
    total = columns * pl.num_programs(0)
    rows = current.shape[0] // nz
    edge = low.shape[0]

    measured, masks, estimates = [], [], []
    for x in range(columns):
        planes = [
            [load_plane(data, data_slabs, x, c, k).T for c in range(coils)] for k in range(2)
        ]
        data_re, data_im = (jnp.concatenate(p, axis=1) for p in planes)
        keep = jnp.where(data_re < sampled_below, 1.0, 0.0)
        measured.append(jnp.concatenate([data_re, data_im], axis=0))
        masks.append(jnp.concatenate([keep, keep], axis=0))
        estimates.append((load(image, x, 0), load(image, x, 1)))
    spectra = [first[x] for x in range(columns)]
    misfits = None
    for repeat in range(2):
        if repeat > 0:
            spectra = [
                to_spectrum(maps, slabs, x, estimates[x], y_right, z_left) for x in range(columns)
            ]
        misfits = [masks[x] * (spectra[x] - measured[x]) for x in range(columns)]
        gradients = [to_gradient(maps, slabs, x, misfits[x], y_back, z_back) for x in range(columns)]
        estimates = [
            tuple(e - step_size * g for e, g in zip(estimates[x], gradients[x]))
            for x in range(columns)
        ]
    for x in range(columns):
        column = step * columns + x
        rounded_parts = [part.astype(jnp.bfloat16) for part in estimates[x]]
        for k in range(2):
            current[pl.ds(k * total + column, nz, stride=rows), :] = estimates[x][k]

        @pl.when(column < edge)
        def _():
            for k in range(2):
                low[column, k] = rounded_parts[k]

        @pl.when(column >= total - edge)
        def _():
            for k in range(2):
                high[column - (total - edge), k] = rounded_parts[k]

        for c in range(coils):
            for k in range(2):
                plane = misfits[x][k * nz : (k + 1) * nz, c * ny : (c + 1) * ny]
                plane = plane.T * wire_scale
                if len(residual.shape) == 6:
                    count, local_ky = residual.shape[1], residual.shape[4]
                    for i in range(count):
                        to = i if c % 2 == 0 else count - 1 - i
                        residual[c, to, x, k] = plane[i * local_ky : (i + 1) * local_ky]
                else:
                    residual[x, c, k] = plane


def column_spec(shape, together):
    return pl.BlockSpec((together,) + shape[1:], lambda i: (i,) + (0,) * (len(shape) - 1))


def fixed_spec(shape):
    return pl.BlockSpec(shape, lambda i: (0,) * len(shape))


def transforms(nz, ny):
    right = {n: jnp.stack(split_constant(complex_matrix(n))) for n in {ny, nz}}
    left = {n: jnp.stack(split_constant(complex_matrix(n).T)) for n in {ny, nz}}
    return right[ny], left[ny], left[nz], right[nz]


def first_spectrum(maps, image, constants, slabs):
    columns, coils, _, nz, ny = maps.shape
    together = math.gcd(columns, 2)
    used = [constants[0], constants[2]]
    shape = (columns, 2 * nz, coils * ny)
    return pl.pallas_call(
        functools.partial(spectrum_kernel, slabs),
        grid=(columns // together,),
        in_specs=[column_spec(maps.shape, together), column_spec(image.shape, together)]
        + [fixed_spec(c.shape) for c in used],
        out_specs=column_spec(shape, together),
        out_shape=jax.ShapeDtypeStruct(shape, jnp.float32),
        name="first_spectrum",
    )(maps, image, *used)


def gradient_steps(maps, image, first, data, constants, rows, slabs, map_slabs, data_slabs):
    columns, coils, _, nz, ny = maps.shape
    together = math.gcd(columns, 2)
    edge = min(3, columns)
    edges = (edge, 2, nz, ny)
    local_ky = ny // slabs
    if data_slabs > 1:
        shape = (coils, slabs, columns, 2, local_ky, nz)
        block = (coils, slabs, together, 2, local_ky, nz)
        residual_spec = pl.BlockSpec(block, lambda i: (0, 0, i, 0, 0, 0))
    else:
        shape = data.shape
        residual_spec = column_spec(shape, together)
    current, low, high, misfit = pl.pallas_call(
        functools.partial(gradient_kernel, map_slabs, data_slabs),
        grid=(columns // together,),
        in_specs=[column_spec(v.shape, together) for v in (maps, image, first, data)]
        + [fixed_spec(c.shape) for c in constants],
        out_specs=[
            fixed_spec((nz * rows, ny)),
            fixed_spec(edges),
            fixed_spec(edges),
            residual_spec,
        ],
        out_shape=[
            jax.ShapeDtypeStruct((nz * rows, ny), jnp.float32),
            jax.ShapeDtypeStruct(edges, jnp.bfloat16),
            jax.ShapeDtypeStruct(edges, jnp.bfloat16),
            jax.ShapeDtypeStruct(shape, jnp.float32),
        ],
        name="gradient_steps",
    )(maps, image, first, data, *constants)
    if misfit.ndim == 5:
        misfit = misfit.reshape(columns, coils, 2, slabs, local_ky, nz).transpose(1, 3, 0, 2, 4, 5)
    return current, low, high, misfit


def row_major(value):
    return with_layout_constraint(value, Layout(major_to_minor=tuple(range(value.ndim))))


def rounded(count, unit):
    return -(-count // unit) * unit


def banded(weight, columns_out, order):
    columns_in = columns_out + 2
    select = np.zeros((3, columns_out, columns_in), np.float32)
    for shift in range(3):
        select[shift, np.arange(columns_out), np.arange(columns_out) + shift] = 1.0
    taps = weight.reshape((3, 3, 3) + weight.shape[1:])
    return jnp.einsum("zyxoj,xab->" + order, taps, jnp.asarray(select, weight.dtype))


def matrices(w_in, w_mid, w_out, columns, block, rows, halo_rows):
    feat = w_mid.shape[1]
    first = banded(w_in, columns + 4, "aozyjb")
    own = first[..., 3 : columns + 3].reshape(-1, 3, 3, 2 * columns)
    own = jnp.pad(own, ((0, 0),) * 3 + ((0, rows - 2 * columns),))
    sides = jnp.concatenate([first[..., :3], first[..., columns + 3 :]], axis=-1)
    sides = jnp.swapaxes(sides, -1, -2).reshape(-1, 3, 3, 12)
    sides = jnp.pad(sides, ((0, 0),) * 3 + ((0, halo_rows - 12),))
    first = jnp.concatenate([own, sides], axis=-1).reshape((columns + 4) * feat, -1)
    middle = banded(w_mid, block, "yaozbj").reshape(3 * block * feat, -1)
    last = banded(w_out, columns, "zyoabj").reshape(9, 2 * columns, -1)
    last = jnp.pad(last, ((0, 0), (0, rows - 2 * columns), (0, 0)))
    return first, middle, last.reshape(9 * rows, -1)


def conv_kernel(place, current, left, right, w_in, w_mid, w_out, packed, pad_0, pad_1, pad_2, halo, refined):
    rows_1, rows_2 = pad_1.shape[1], pad_2.shape[1]
    nz, ny = refined.shape[0], refined.shape[2]
    rows = refined.shape[1]
    halo_rows = halo.shape[0] // nz
    bf16, f32 = jnp.bfloat16, jnp.float32

    for ref in (pad_0, pad_1):
        empty = jnp.zeros(ref.shape[1:], ref.dtype)
        ref[0] = empty
        ref[nz + 1] = empty

    def shifted(value, by):
        lane = lax.broadcasted_iota(jnp.int32, value.shape, 1)
        edge = 0 if by == 1 else ny - 1
        return jnp.where(lane == edge, 0.0, pltpu.roll(value, by % ny, 1))

    def inside(count, before):
        feat = (rows_1 - rows_2) // 2
        row = lax.broadcasted_iota(jnp.int32, (count, ny), 0)
        x = place[0] - before + row // feat
        return jnp.where((x >= 0) & (x < place[1]), 1.0, 0.0)

    keep_1, keep_2 = inside(rows_1, 2), inside(rows_2, 1)

    for side, ref in enumerate((left, right)):
        for column in range(3):
            for k in range(2):
                row = 6 * side + 2 * column + k
                halo[pl.ds(row, nz, stride=halo_rows), :] = ref[column, k].astype(f32)
    for row in range(12, halo_rows):
        halo[pl.ds(row, nz, stride=halo_rows), :] = jnp.zeros((nz, ny), f32)

    def spread(z, carry):
        own = current[pl.ds(pl.multiple_of(z * rows, 8), rows), :]
        sides = halo[pl.ds(pl.multiple_of(z * halo_rows, 8), halo_rows), :]
        value = jnp.concatenate([own, sides], axis=0)
        shifts = [shifted(value, 1), value, shifted(value, -1)]
        pad_0[z + 1] = jnp.concatenate(shifts, axis=0).astype(bf16)
        return carry

    def pair(block):
        near = jnp.concatenate([block[0], block[1], block[2]], axis=0)
        far = jnp.concatenate([block[1], block[2], block[3]], axis=0)
        return jnp.concatenate([near, far], axis=1)

    def first(i):
        out = dot(w_in[...], pair(pad_0[pl.ds(2 * i, 4)]))
        for k in range(2):
            part = jnp.maximum(out[:, k * ny : (k + 1) * ny], 0.0) * keep_1
            pad_1[2 * i + k + 1] = part.astype(bf16)

    block_out = w_mid.shape[0] // 3
    block_in = w_mid.shape[1] // 3

    def middle(i):
        for b in range(rows_2 // block_out):
            low = b * block_out
            out = dot(w_mid[...], pair(pad_1[pl.ds(2 * i, 4), low : low + block_in]))
            for k in range(2):
                part = out[:, k * ny : (k + 1) * ny]
                total = part[block_out : 2 * block_out]
                total = total + shifted(part[:block_out], 1)
                total = total + shifted(part[2 * block_out :], -1)
                total = jnp.maximum(total, 0.0) * keep_2[low : low + block_out]
                pad_2[2 * i + k, low : low + block_out] = total.astype(bf16)

    def finish(z, total, largest):
        out = total[rows : 2 * rows]
        out = out + shifted(total[:rows], 1) + shifted(total[2 * rows :], -1)
        out = out + current[pl.ds(pl.multiple_of(z * rows, 8), rows), :]
        refined[z] = out
        return jnp.maximum(largest, jnp.abs(out))

    def last(i, carry):
        older, newer, largest = carry
        both = jnp.concatenate([pad_2[2 * i], pad_2[2 * i + 1]], axis=1)
        out = dot(w_out[...], both)
        for k in range(2):
            part = out[:, k * ny : (k + 1) * ny]
            z = 2 * i + k - 1
            total = older + part[6 * rows :]
            if k == 0:
                total = jnp.where(i > 0, total, 0.0)
            largest = finish(jnp.maximum(z, 0), total, largest)
            older, newer = newer + part[3 * rows : 6 * rows], part[: 3 * rows]
        return older, newer, largest

    lax.fori_loop(0, nz, spread, 0, unroll=4)

    def alone(step):
        def run(i, carry):
            step(i)
            return carry

        return run

    lax.fori_loop(0, nz // 2, alone(first), 0, unroll=4)
    lax.fori_loop(0, nz // 2, alone(middle), 0, unroll=8)
    sums = jnp.zeros((3 * rows, ny), f32)
    carry = (sums, sums, jnp.zeros((rows, ny), f32))
    older, _, largest = lax.fori_loop(0, nz // 2, last, carry, unroll=4)
    largest = finish(nz - 1, older, largest)

    if packed.dtype != jnp.int16:
        packed[...] = refined[...]
        return

    groups, slabs = packed.shape[:2]
    columns = rows // 2
    top = jnp.maximum(jnp.max(largest, axis=(0, 1), keepdims=True), 1e-30)
    code = jnp.ceil(jnp.log(top * (1.0 / 32000.0)) * (steps_per_octave / math.log(2.0)))
    factor = jnp.exp(code * (-math.log(2.0) / steps_per_octave))
    lane = lax.broadcasted_iota(jnp.int32, (columns, ny), 1)
    bias = (code + code_bias).astype(jnp.int32)
    bits = jnp.broadcast_to(bias, (16, ny)) >> lax.broadcasted_iota(jnp.int32, (16, ny), 0)
    bits = bits & 1

    def pack(s, carry):
        for z in range(0, nz // slabs, 2):
            halves = [[], []]
            for k in range(2):
                value = refined[s * (nz // slabs) + z + k] * (factor * (0.5 if z == 0 else 1.0))
                value = jnp.round(value)
                re, im = value[:columns], value[columns:]
                halves[0].append(jnp.where(lane < ny // 2, re, pltpu.roll(im, ny // 2, 1)))
                halves[1].append(jnp.where(lane < ny // 2, pltpu.roll(re, ny // 2, 1), im))
            for c in range(2):
                both = jnp.concatenate(halves[c], axis=0).astype(jnp.int32)
                if z == 0:
                    both = 2 * both + bits
                to = s if c == 0 else slabs - 1 - s
                packed[c, to, z * columns : (z + 2) * columns] = both.astype(jnp.int16)
        return carry

    lax.fori_loop(0, slabs, pack, 0)


def denoise(place, current, left, right, weights, out_shape):
    w_in, w_mid, w_out = weights
    nz, ny = left.shape[2:]
    rows = current.shape[0] // nz
    halo_rows = w_in.shape[1] // 9 - rows
    flops = nz * ny * sum(2 * m.shape[0] * m.shape[1] for m in weights)
    return pl.pallas_call(
        conv_kernel,
        in_specs=[pl.BlockSpec(memory_space=pltpu.SMEM)]
        + [pl.BlockSpec(memory_space=pltpu.VMEM)] * 6,
        out_specs=pl.BlockSpec(memory_space=pltpu.VMEM),
        out_shape=out_shape,
        scratch_shapes=[
            pltpu.VMEM((nz + 2, w_in.shape[1] // 3, ny), jnp.bfloat16),
            pltpu.VMEM((nz + 2, w_in.shape[0], ny), jnp.bfloat16),
            pltpu.VMEM((nz, w_out.shape[1], ny), jnp.bfloat16),
            pltpu.VMEM((nz * halo_rows, ny), jnp.float32),
            pltpu.VMEM((nz, rows, ny), jnp.float32),
        ],
        cost_estimate=pl.CostEstimate(
            flops=flops, transcendentals=0, bytes_accessed=8 * current.size
        ),
        name="denoise",
    )(place, current, left, right, w_in, w_mid, w_out)


def unpack_kernel(values, tag, out):
    devices, both, lanes = values.shape
    columns = both // 2
    bits = tag[...].astype(jnp.int32) & 1
    bits = bits << lax.broadcasted_iota(jnp.int32, bits.shape, 1)
    code = jnp.sum(bits.astype(jnp.float32), axis=1, keepdims=True) - code_bias
    factor = jnp.exp(code * (math.log(2.0) / steps_per_octave))
    value = values[...].astype(jnp.int32).astype(jnp.float32) * factor
    for k in range(2):
        plane = value[:, k * columns : (k + 1) * columns].reshape(devices * columns, lanes)
        plane = plane.T
        out[0, k] = plane[: lanes // 2]
        out[1, k] = plane[lanes // 2 :]


def unpack(sent, columns, local_z):
    devices, _, lanes = sent.shape
    return pl.pallas_call(
        unpack_kernel,
        grid=(local_z // 2,),
        in_specs=[
            pl.BlockSpec((devices, 2 * columns, lanes), lambda i: (0, i, 0)),
            pl.BlockSpec((devices, 16, lanes), lambda i: (0, 0, 0)),
        ],
        out_specs=pl.BlockSpec((2, 2, lanes // 2, devices * columns), lambda i: (0, i, 0, 0)),
        out_shape=jax.ShapeDtypeStruct(
            (2, local_z, lanes // 2, devices * columns), jnp.float32
        ),
        name="unpack",
    )(sent, sent)


def chain(slabs, groups):
    pairs = []
    for c in range(groups):
        run = range(slabs) if c % 2 == 0 else reversed(range(slabs))
        pairs.extend((s, c) for s in run)
    return pairs


def exchange(value, slabs, groups):
    order = [[c * slabs + s for s, c in chain(slabs, groups)]]
    return lax.all_to_all(value, AXES, 0, 0, tiled=True, axis_index_groups=order)


def unfold(value):
    groups = value.shape[0]
    return jnp.stack([value[c] if c % 2 == 0 else jnp.flip(value[c], 0) for c in range(groups)])


def neighbours(low, high, slabs, groups):
    devices = slabs * groups
    columns = low.shape[0]
    place = [s * groups + c for s, c in chain(slabs, groups)]
    left, right, found, hop = [], [], 0, 1
    while found < 3:
        count = min(columns, 3 - found)
        up = [(place[i], place[i + hop]) for i in range(devices - hop)]
        down = [(j, i) for i, j in up]
        left.insert(0, lax.ppermute(high[columns - count :], ("slab", "coil"), up))
        right.append(lax.ppermute(low[:count], ("slab", "coil"), down))
        found += count
        hop += 1
    return jnp.concatenate(left, axis=0), jnp.concatenate(right, axis=0)


def shards(image, sensitivity, kspace, sampled, w_in, w_mid, w_out):
    slabs, groups = lax.axis_size("slab"), lax.axis_size("coil")
    devices = slabs * groups
    _, local_z, ny, nx = image.shape
    local_coils = sensitivity.shape[1]
    coils = local_coils * groups
    nz, local_ky = kspace.shape[2:4]
    columns = nx // devices
    local_y = ny // groups

    f32 = jnp.float32
    parts = math.gcd(local_z, groups)
    share = local_z // parts
    own = lax.dynamic_slice_in_dim(image, lax.axis_index("coil") % parts * share, share, 1)
    sent = [v.reshape(-1, ny, nx).astype(wire) for v in (sensitivity, own)]
    sent = lax.optimization_barrier(jnp.concatenate(sent, axis=0))
    sent = exchange(sent.transpose(2, 0, 1), slabs, groups)

    rows = rounded(2 * columns, 8)
    halo_rows = rounded(rows + 12, 16) - rows
    block = (columns + 2) // math.gcd(columns + 2, 2)
    weights = matrices(w_in, w_mid, w_out, columns, block, rows, halo_rows)
    slab, group = lax.axis_index("slab"), lax.axis_index("coil")
    chunk = group * slabs + jnp.where(group % 2 == 0, slab, slabs - 1 - slab)
    place = jnp.stack([chunk * columns, jnp.int32(nx)])
    re_x, im_x = (jnp.asarray(v, f32) for v in dft(nx))
    re_x, im_x = lax.optimization_barrier((re_x, im_x))
    transform_x = jnp.stack([re_x, im_x, -im_x, re_x]).reshape(2, 2, nx, nx)
    data = jnp.einsum("aczyr,baxr->xcbyz", kspace, transform_x, precision=three_pass)
    data = jnp.where(sampled.T[None, None, None] > 0, data, not_sampled).astype(wire)
    data = row_major(data)
    weights = [row_major(w) for w in weights]
    sent, data, weights, place = lax.optimization_barrier((sent, data, weights, place))

    data = exchange(data, slabs, groups)
    cut = 2 * local_coils * local_z
    maps = sent[:, :cut].reshape(groups, slabs, columns, 2, local_coils, local_z, ny)
    map_slabs = 1 if local_z % 8 > 0 or local_coils > 1 else slabs
    data_slabs = 1 if local_ky % 8 > 0 or local_coils > 1 else slabs
    if map_slabs == 1:
        maps = unfold(maps)
    maps = maps.transpose(2, 0, 4, 3, 1, 5, 6).reshape(columns, coils, 2, nz, ny).astype(f32)
    own = unfold(sent[:, cut:].reshape(groups, slabs, columns, 2, share, ny)[:parts])
    own = own.transpose(2, 3, 1, 0, 4, 5).reshape(columns, 2, nz, ny).astype(f32)
    constants = transforms(nz, ny)
    first = first_spectrum(maps, own, constants, map_slabs)
    data, first = lax.optimization_barrier((data, first))
    data = data.reshape(groups, slabs, columns, local_coils, 2, local_ky, nz)
    if data_slabs == 1:
        data = unfold(data)
    data = data.transpose(2, 0, 3, 4, 1, 5, 6).reshape(columns, coils, 2, ny, nz)
    current, low, high, misfit = gradient_steps(
        maps, own, first, data.astype(f32), constants, rows, slabs, map_slabs, data_slabs
    )
    if rows > 2 * columns:
        used = jnp.arange(rows, dtype=jnp.int32)[:, None] < 2 * columns
        current = jnp.where(used, current.reshape(nz, rows, ny), 0.0).reshape(-1, ny)

    received = neighbours(low, high, slabs, groups)
    misfit = misfit.astype(wire).reshape(groups, local_coils, slabs, columns, 2, local_ky, nz)
    misfit = misfit.transpose(0, 2, 3, 1, 4, 5, 6)
    if data_slabs == 1:
        misfit = unfold(misfit)
    misfit = misfit.reshape(devices, columns, local_coils, 2, local_ky, nz)
    received, misfit = lax.optimization_barrier((received, misfit))
    misfit = exchange(misfit, slabs, groups)

    aligned = columns == 8 and local_z % 2 == 0 and ny == 128 and groups == 2
    if aligned:
        shape = (groups, slabs, local_z * columns, ny)
        out_shape = jax.ShapeDtypeStruct(shape, jnp.int16)
    else:
        out_shape = jax.ShapeDtypeStruct((nz, rows, ny), f32)
    refined = denoise(place, current, *received, weights, out_shape)
    refined, misfit = lax.optimization_barrier((refined, misfit))

    misfit = misfit.astype(f32).reshape(nx, local_coils, 2, local_ky, nz) * (1.0 / wire_scale)
    residual = jnp.einsum("xcayz,abxr->bczyr", misfit, transform_x, precision=three_pass)

    if aligned:
        sent = refined.reshape(devices, -1, ny)
        sent = exchange(sent, slabs, groups)
        return unpack(sent, columns, local_z), residual
    refined = refined[:, : 2 * columns].reshape(nz, 2, columns, ny)
    largest = jnp.maximum(jnp.max(jnp.abs(refined)), 1e-30)
    exponent = jnp.ceil(jnp.log2(largest)) - 15.0
    sent = (refined * jnp.exp2(-exponent)).astype(wire)
    sent = sent.reshape(slabs, local_z, 2, columns, groups, local_y)
    sent = unfold(sent.transpose(4, 0, 3, 2, 1, 5))
    sent = sent.reshape(devices, columns, 2 * local_z * local_y)
    tag = jnp.broadcast_to(exponent.astype(wire), (devices, columns, ny))
    sent = jnp.concatenate([sent, tag], axis=2)
    sent = exchange(sent, slabs, groups)
    scale = jnp.exp2(sent[:, :, -1].astype(f32)).reshape(nx)
    refined = sent[:, :, :-ny].reshape(nx, 2, local_z, local_y).astype(f32)
    refined = refined.transpose(1, 2, 3, 0) * scale
    return (refined, residual)


def solution(mesh):
    placed = (
        P(None, "slab", None, None),
        P(None, "coil", "slab", None, None),
        P(None, "coil", None, "slab", None),
        P(None, "slab"),
        P(),
        P(),
        P(),
    )
    return jax.shard_map(
        shards,
        mesh=mesh,
        in_specs=placed,
        out_specs=(P(None, "slab", "coil", None), P(None, "coil", None, "slab", None)),
        check_vma=False,
    )
```

```python
import functools
import math

import jax
import jax.numpy as jnp
import numpy as np
from jax import lax
from jax.experimental import pallas as pl
from jax.experimental.layout import Layout, with_layout_constraint
from jax.experimental.pallas import tpu as pltpu
from jax.sharding import PartitionSpec as P

AXES = ("coil", "slab")
step_size = 0.5
three_pass = lax.Precision.HIGH
wire = jnp.float16
wire_scale = 2.0**-6
not_sampled = 60000.0
sampled_below = 30000.0
steps_per_octave = 64.0
code_bias = 8192.0


def dft(length):
    index = np.arange(length)
    angles = (index[:, None] * index[None, :] % length) * (2.0 * math.pi / length)
    factor = 1.0 / math.sqrt(length)
    return np.cos(angles) * factor, -np.sin(angles) * factor


def split_constant(value):
    value = jnp.asarray(value, jnp.float32)
    high = value.astype(jnp.bfloat16)
    return high, (value - high.astype(jnp.float32)).astype(jnp.bfloat16)


def complex_matrix(length):
    re, im = dft(length)
    return np.block([[re, im], [-im, re]])


def split(value):
    high = value.astype(jnp.bfloat16)
    low = (value - high.astype(jnp.float32)).astype(jnp.bfloat16)
    return high, low


def dot(a, b):
    return jnp.dot(a, b, preferred_element_type=jnp.float32)


def from_right(value, matrix):
    high, low = split(value)
    rows = value.shape[0]
    both = dot(jnp.concatenate([high, low], axis=0), matrix[0])
    return both[:rows] + both[rows:] + dot(high, matrix[1])


def from_left(matrix, value):
    high, low = split(value)
    rows = matrix.shape[1]
    both = dot(matrix[...].reshape(2 * rows, matrix.shape[2]), high)
    return both[:rows] + both[rows:] + dot(matrix[0], low)


def load(ref, *index):
    return ref[index].astype(jnp.float32)


def load_plane(ref, slabs, *index):
    plane = load(ref, *index)
    block = plane.shape[0] // slabs
    if slabs > 1 and index[1] % 2 == 1:
        parts = [plane[s * block : (s + 1) * block] for s in reversed(range(slabs))]
        plane = jnp.concatenate(parts, axis=0)
    return plane


def load_lines(ref, slabs, x, c):
    if slabs == 1:
        re, im = load(ref, x, c, 0), load(ref, x, c, 1)
        return re, im, jnp.where(re < sampled_below, 1.0, 0.0)
    senders = list(range(slabs)) if c % 2 == 0 else list(reversed(range(slabs)))

    def plane(k):
        blocks = [ref[c * slabs + s, x, k].astype(jnp.int32) for s in senders]
        return jnp.concatenate(blocks, axis=0)

    re, im = plane(0), plane(1)
    scale = scale_of(read_code(re))
    keep = jnp.where(re > -32766, 1.0, 0.0)
    return re.astype(jnp.float32) * scale, im.astype(jnp.float32) * scale, keep


def scale_code(largest):
    top = jnp.maximum(largest, 1e-30) * (1.0 / 32000.0)
    return jnp.ceil(jnp.log(top) * (steps_per_octave / math.log(2.0)))


def scale_of(code):
    return jnp.exp(code * (math.log(2.0) / steps_per_octave))


def low_bits(code, shape, axis):
    bias = jnp.broadcast_to((code + code_bias).astype(jnp.int32), shape)
    return (bias >> (lax.broadcasted_iota(jnp.int32, shape, axis) & 15)) & 1


def read_code(value):
    lane = lax.broadcasted_iota(jnp.int32, value.shape, value.ndim - 1)
    bits = jnp.where(lane < 16, (value & 1) << (lane & 15), 0).astype(jnp.float32)
    return jnp.sum(bits, axis=-1, keepdims=True) - code_bias


def to_spectrum(maps, slabs, x, estimate, y_right, z_left):
    coils, _, nz, ny = maps.shape[1:]
    cur_re, cur_im = estimate
    pieces = []
    for c in range(coils):
        map_re, map_im = (load_plane(maps, slabs, x, c, k) for k in range(2))
        coil_re = map_re * cur_re - map_im * cur_im
        coil_im = map_re * cur_im + map_im * cur_re
        pieces.append(jnp.concatenate([coil_re, coil_im], axis=1))
    over_y = from_right(jnp.concatenate(pieces, axis=0), y_right)
    planes = [over_y[c * nz : (c + 1) * nz] for c in range(coils)]
    upper = jnp.concatenate([p[:, :ny] for p in planes], axis=1)
    lower = jnp.concatenate([p[:, ny:] for p in planes], axis=1)
    return from_left(z_left, jnp.concatenate([upper, lower], axis=0))


def to_gradient(maps, slabs, x, misfit, y_back, z_back):
    coils, _, nz, ny = maps.shape[1:]
    over_z = from_left(z_back, misfit)
    pieces = []
    for c in range(coils):
        lanes = slice(c * ny, (c + 1) * ny)
        pieces.append(jnp.concatenate([over_z[:nz, lanes], over_z[nz:, lanes]], axis=1))
    back = from_right(jnp.concatenate(pieces, axis=0), y_back)
    grad_re = jnp.zeros((nz, ny), jnp.float32)
    grad_im = jnp.zeros((nz, ny), jnp.float32)
    for c in range(coils):
        map_re, map_im = (load_plane(maps, slabs, x, c, k) for k in range(2))
        back_re = back[c * nz : (c + 1) * nz, :ny]
        back_im = back[c * nz : (c + 1) * nz, ny:]
        grad_re += map_re * back_re + map_im * back_im
        grad_im += map_re * back_im - map_im * back_re
    return grad_re, grad_im


def spectrum_kernel(slabs, maps, image, y_right, z_left, spectrum):
    for x in range(maps.shape[0]):
        estimate = (load(image, x, 0), load(image, x, 1))
        spectrum[x] = to_spectrum(maps, slabs, x, estimate, y_right, z_left)


def gradient_kernel(slabs, data_slabs, maps, image, first, data, y_right, y_back, z_left, z_back, current, low, high, residual):
    columns, coils, _, nz, ny = maps.shape
    step = pl.program_id(0)
    total = columns * pl.num_programs(0)
    rows = current.shape[0] // nz
    edge = low.shape[0]

    measured, masks, estimates = [], [], []
    for x in range(columns):
        lines = [[v.T for v in load_lines(data, data_slabs, x, c)] for c in range(coils)]
        data_re, data_im, keep = (jnp.concatenate(v, axis=1) for v in zip(*lines))
        measured.append(jnp.concatenate([data_re, data_im], axis=0))
        masks.append(jnp.concatenate([keep, keep], axis=0))
        estimates.append((load(image, x, 0), load(image, x, 1)))
    spectra = [first[x] for x in range(columns)]
    misfits = None
    for repeat in range(2):
        if repeat > 0:
            spectra = [
                to_spectrum(maps, slabs, x, estimates[x], y_right, z_left) for x in range(columns)
            ]
        misfits = [masks[x] * (spectra[x] - measured[x]) for x in range(columns)]
        gradients = [to_gradient(maps, slabs, x, misfits[x], y_back, z_back) for x in range(columns)]
        estimates = [
            tuple(e - step_size * g for e, g in zip(estimates[x], gradients[x]))
            for x in range(columns)
        ]
    for x in range(columns):
        column = step * columns + x
        rounded_parts = [part.astype(jnp.bfloat16) for part in estimates[x]]
        for k in range(2):
            current[pl.ds(k * total + column, nz, stride=rows), :] = estimates[x][k]

        @pl.when(column < edge)
        def _():
            for k in range(2):
                low[column, k] = rounded_parts[k]

        @pl.when(column >= total - edge)
        def _():
            for k in range(2):
                high[column - (total - edge), k] = rounded_parts[k]

        for c in range(coils):
            lanes = slice(c * ny, (c + 1) * ny)
            planes = [misfits[x][k * nz : (k + 1) * nz, lanes].T for k in range(2)]
            if data_slabs == 1:
                for k in range(2):
                    residual[x, c, k] = planes[k] * wire_scale
                continue
            largest = jnp.maximum(jnp.abs(planes[0]), jnp.abs(planes[1]))
            code = scale_code(jnp.max(largest, axis=1, keepdims=True))
            half = 0.5 / scale_of(code)
            bits = low_bits(code, (ny, nz), 1)
            local_ky = ny // data_slabs
            for k in range(2):
                plane = 2 * jnp.round(planes[k] * half).astype(jnp.int32) + bits
                plane = plane.astype(jnp.int16)
                for i in range(data_slabs):
                    to = i if c % 2 == 0 else data_slabs - 1 - i
                    residual[c, to, x, k] = plane[i * local_ky : (i + 1) * local_ky]


def column_spec(shape, together):
    return pl.BlockSpec((together,) + shape[1:], lambda i: (i,) + (0,) * (len(shape) - 1))


def fixed_spec(shape):
    return pl.BlockSpec(shape, lambda i: (0,) * len(shape))


def transforms(nz, ny):
    right = {n: jnp.stack(split_constant(complex_matrix(n))) for n in {ny, nz}}
    left = {n: jnp.stack(split_constant(complex_matrix(n).T)) for n in {ny, nz}}
    return right[ny], left[ny], left[nz], right[nz]


def first_spectrum(maps, image, constants, slabs):
    columns, coils, _, nz, ny = maps.shape
    together = math.gcd(columns, 2)
    used = [constants[0], constants[2]]
    shape = (columns, 2 * nz, coils * ny)
    return pl.pallas_call(
        functools.partial(spectrum_kernel, slabs),
        grid=(columns // together,),
        in_specs=[column_spec(maps.shape, together), column_spec(image.shape, together)]
        + [fixed_spec(c.shape) for c in used],
        out_specs=column_spec(shape, together),
        out_shape=jax.ShapeDtypeStruct(shape, jnp.float32),
        name="first_spectrum",
    )(maps, image, *used)


def gradient_steps(maps, image, first, data, constants, rows, slabs, map_slabs, data_slabs):
    columns, coils, _, nz, ny = maps.shape
    together = math.gcd(columns, 2)
    edge = min(3, columns)
    edges = (edge, 2, nz, ny)
    local_ky = ny // slabs
    if data_slabs > 1:
        shape = (coils, slabs, columns, 2, local_ky, nz)
        block = (coils, slabs, together, 2, local_ky, nz)
        residual_spec = pl.BlockSpec(block, lambda i: (0, 0, i, 0, 0, 0))
        block = (coils * slabs, together, 2, local_ky, nz)
        data_spec = pl.BlockSpec(block, lambda i: (0, i, 0, 0, 0))
    else:
        shape = data.shape
        residual_spec = data_spec = column_spec(shape, together)
    current, low, high, misfit = pl.pallas_call(
        functools.partial(gradient_kernel, map_slabs, data_slabs),
        grid=(columns // together,),
        in_specs=[column_spec(v.shape, together) for v in (maps, image, first)]
        + [data_spec]
        + [fixed_spec(c.shape) for c in constants],
        out_specs=[
            fixed_spec((nz * rows, ny)),
            fixed_spec(edges),
            fixed_spec(edges),
            residual_spec,
        ],
        out_shape=[
            jax.ShapeDtypeStruct((nz * rows, ny), jnp.float32),
            jax.ShapeDtypeStruct(edges, jnp.bfloat16),
            jax.ShapeDtypeStruct(edges, jnp.bfloat16),
            jax.ShapeDtypeStruct(shape, jnp.int16 if data_slabs > 1 else jnp.float32),
        ],
        name="gradient_steps",
    )(maps, image, first, data, *constants)
    if misfit.ndim == 5:
        misfit = misfit.reshape(columns, coils, 2, slabs, local_ky, nz).transpose(1, 3, 0, 2, 4, 5)
    return current, low, high, misfit


def row_major(value):
    return with_layout_constraint(value, Layout(major_to_minor=tuple(range(value.ndim))))


def rounded(count, unit):
    return -(-count // unit) * unit


def banded(weight, columns_out, order):
    columns_in = columns_out + 2
    select = np.zeros((3, columns_out, columns_in), np.float32)
    for shift in range(3):
        select[shift, np.arange(columns_out), np.arange(columns_out) + shift] = 1.0
    taps = weight.reshape((3, 3, 3) + weight.shape[1:])
    return jnp.einsum("zyxoj,xab->" + order, taps, jnp.asarray(select, weight.dtype))


def matrices(w_in, w_mid, w_out, columns, block, rows, halo_rows):
    feat = w_mid.shape[1]
    first = banded(w_in, columns + 4, "aozyjb")
    own = first[..., 3 : columns + 3].reshape(-1, 3, 3, 2 * columns)
    own = jnp.pad(own, ((0, 0),) * 3 + ((0, rows - 2 * columns),))
    sides = jnp.concatenate([first[..., :3], first[..., columns + 3 :]], axis=-1)
    sides = jnp.swapaxes(sides, -1, -2).reshape(-1, 3, 3, 12)
    sides = jnp.pad(sides, ((0, 0),) * 3 + ((0, halo_rows - 12),))
    first = jnp.concatenate([own, sides], axis=-1).reshape((columns + 4) * feat, -1)
    middle = banded(w_mid, block, "yaozbj").reshape(3 * block * feat, -1)
    last = banded(w_out, columns, "zyoabj").reshape(9, 2 * columns, -1)
    last = jnp.pad(last, ((0, 0), (0, rows - 2 * columns), (0, 0)))
    return first, middle, last.reshape(9 * rows, -1)


def conv_kernel(place, current, left, right, w_in, w_mid, w_out, packed, pad_0, pad_1, pad_2, halo, refined):
    rows_1, rows_2 = pad_1.shape[1], pad_2.shape[1]
    nz, ny = refined.shape[0], refined.shape[2]
    rows = refined.shape[1]
    halo_rows = halo.shape[0] // nz
    bf16, f32 = jnp.bfloat16, jnp.float32

    for ref in (pad_0, pad_1):
        empty = jnp.zeros(ref.shape[1:], ref.dtype)
        ref[0] = empty
        ref[nz + 1] = empty

    def shifted(value, by):
        lane = lax.broadcasted_iota(jnp.int32, value.shape, 1)
        edge = 0 if by == 1 else ny - 1
        return jnp.where(lane == edge, 0.0, pltpu.roll(value, by % ny, 1))

    def inside(count, before):
        feat = (rows_1 - rows_2) // 2
        row = lax.broadcasted_iota(jnp.int32, (count, ny), 0)
        x = place[0] - before + row // feat
        return jnp.where((x >= 0) & (x < place[1]), 1.0, 0.0)

    keep_1, keep_2 = inside(rows_1, 2), inside(rows_2, 1)

    for side, ref in enumerate((left, right)):
        for column in range(3):
            for k in range(2):
                row = 6 * side + 2 * column + k
                halo[pl.ds(row, nz, stride=halo_rows), :] = ref[column, k].astype(f32)
    for row in range(12, halo_rows):
        halo[pl.ds(row, nz, stride=halo_rows), :] = jnp.zeros((nz, ny), f32)

    def spread(z, carry):
        own = current[pl.ds(pl.multiple_of(z * rows, 8), rows), :]
        sides = halo[pl.ds(pl.multiple_of(z * halo_rows, 8), halo_rows), :]
        value = jnp.concatenate([own, sides], axis=0)
        shifts = [shifted(value, 1), value, shifted(value, -1)]
        pad_0[z + 1] = jnp.concatenate(shifts, axis=0).astype(bf16)
        return carry

    def pair(block):
        near = jnp.concatenate([block[0], block[1], block[2]], axis=0)
        far = jnp.concatenate([block[1], block[2], block[3]], axis=0)
        return jnp.concatenate([near, far], axis=1)

    def first(i):
        out = dot(w_in[...], pair(pad_0[pl.ds(2 * i, 4)]))
        for k in range(2):
            part = jnp.maximum(out[:, k * ny : (k + 1) * ny], 0.0) * keep_1
            pad_1[2 * i + k + 1] = part.astype(bf16)

    block_out = w_mid.shape[0] // 3
    block_in = w_mid.shape[1] // 3

    def middle(i):
        for b in range(rows_2 // block_out):
            low = b * block_out
            out = dot(w_mid[...], pair(pad_1[pl.ds(2 * i, 4), low : low + block_in]))
            for k in range(2):
                part = out[:, k * ny : (k + 1) * ny]
                total = part[block_out : 2 * block_out]
                total = total + shifted(part[:block_out], 1)
                total = total + shifted(part[2 * block_out :], -1)
                total = jnp.maximum(total, 0.0) * keep_2[low : low + block_out]
                pad_2[2 * i + k, low : low + block_out] = total.astype(bf16)

    def finish(z, total, largest):
        out = total[rows : 2 * rows]
        out = out + shifted(total[:rows], 1) + shifted(total[2 * rows :], -1)
        out = out + current[pl.ds(pl.multiple_of(z * rows, 8), rows), :]
        refined[z] = out
        return jnp.maximum(largest, jnp.abs(out))

    def last(i, carry):
        older, newer, largest = carry
        both = jnp.concatenate([pad_2[2 * i], pad_2[2 * i + 1]], axis=1)
        out = dot(w_out[...], both)
        for k in range(2):
            part = out[:, k * ny : (k + 1) * ny]
            z = 2 * i + k - 1
            total = older + part[6 * rows :]
            if k == 0:
                total = jnp.where(i > 0, total, 0.0)
            largest = finish(jnp.maximum(z, 0), total, largest)
            older, newer = newer + part[3 * rows : 6 * rows], part[: 3 * rows]
        return older, newer, largest

    lax.fori_loop(0, nz, spread, 0, unroll=4)

    def alone(step):
        def run(i, carry):
            step(i)
            return carry

        return run

    lax.fori_loop(0, nz // 2, alone(first), 0, unroll=8)
    lax.fori_loop(0, nz // 2, alone(middle), 0, unroll=8)
    sums = jnp.zeros((3 * rows, ny), f32)
    carry = (sums, sums, jnp.zeros((rows, ny), f32))
    older, _, largest = lax.fori_loop(0, nz // 2, last, carry, unroll=8)
    largest = finish(nz - 1, older, largest)

    if packed.dtype != jnp.int16:
        packed[...] = refined[...]
        return

    groups, slabs = packed.shape[:2]
    columns = rows // 2
    code = scale_code(jnp.max(largest, axis=(0, 1), keepdims=True))
    factor = 1.0 / scale_of(code)
    lane = lax.broadcasted_iota(jnp.int32, (columns, ny), 1)
    bits = low_bits(code, (16, ny), 0)

    def pack(s, carry):
        for z in range(0, nz // slabs, 2):
            halves = [[], []]
            for k in range(2):
                value = refined[s * (nz // slabs) + z + k] * (factor * (0.5 if z == 0 else 1.0))
                value = jnp.round(value)
                re, im = value[:columns], value[columns:]
                halves[0].append(jnp.where(lane < ny // 2, re, pltpu.roll(im, ny // 2, 1)))
                halves[1].append(jnp.where(lane < ny // 2, pltpu.roll(re, ny // 2, 1), im))
            for c in range(2):
                both = jnp.concatenate(halves[c], axis=0).astype(jnp.int32)
                if z == 0:
                    both = 2 * both + bits
                to = s if c == 0 else slabs - 1 - s
                packed[c, to, z * columns : (z + 2) * columns] = both.astype(jnp.int16)
        return carry

    lax.fori_loop(0, slabs, pack, 0)


def denoise(place, current, left, right, weights, out_shape):
    w_in, w_mid, w_out = weights
    nz, ny = left.shape[2:]
    rows = current.shape[0] // nz
    halo_rows = w_in.shape[1] // 9 - rows
    flops = nz * ny * sum(2 * m.shape[0] * m.shape[1] for m in weights)
    return pl.pallas_call(
        conv_kernel,
        in_specs=[pl.BlockSpec(memory_space=pltpu.SMEM)]
        + [pl.BlockSpec(memory_space=pltpu.VMEM)] * 6,
        out_specs=pl.BlockSpec(memory_space=pltpu.VMEM),
        out_shape=out_shape,
        scratch_shapes=[
            pltpu.VMEM((nz + 2, w_in.shape[1] // 3, ny), jnp.bfloat16),
            pltpu.VMEM((nz + 2, w_in.shape[0], ny), jnp.bfloat16),
            pltpu.VMEM((nz, w_out.shape[1], ny), jnp.bfloat16),
            pltpu.VMEM((nz * halo_rows, ny), jnp.float32),
            pltpu.VMEM((nz, rows, ny), jnp.float32),
        ],
        cost_estimate=pl.CostEstimate(
            flops=flops, transcendentals=0, bytes_accessed=8 * current.size
        ),
        name="denoise",
    )(place, current, left, right, w_in, w_mid, w_out)


def unpack_kernel(values, tag, out):
    devices, both, lanes = values.shape
    columns = both // 2
    bits = tag[...].astype(jnp.int32) & 1
    bits = bits << lax.broadcasted_iota(jnp.int32, bits.shape, 1)
    code = jnp.sum(bits.astype(jnp.float32), axis=1, keepdims=True) - code_bias
    factor = scale_of(code)
    value = values[...].astype(jnp.int32).astype(jnp.float32) * factor
    for k in range(2):
        plane = value[:, k * columns : (k + 1) * columns].reshape(devices * columns, lanes)
        plane = plane.T
        out[0, k] = plane[: lanes // 2]
        out[1, k] = plane[lanes // 2 :]


def unpack(sent, columns, local_z):
    devices, _, lanes = sent.shape
    some = devices
    return pl.pallas_call(
        unpack_kernel,
        grid=(local_z // 2, devices // some),
        in_specs=[
            pl.BlockSpec((some, 2 * columns, lanes), lambda i, j: (j, i, 0)),
            pl.BlockSpec((some, 16, lanes), lambda i, j: (j, 0, 0)),
        ],
        out_specs=pl.BlockSpec((2, 2, lanes // 2, some * columns), lambda i, j: (0, i, 0, j)),
        out_shape=jax.ShapeDtypeStruct(
            (2, local_z, lanes // 2, devices * columns), jnp.float32
        ),
        name="unpack",
    )(sent, sent)


def chain(slabs, groups):
    pairs = []
    for c in range(groups):
        run = range(slabs) if c % 2 == 0 else reversed(range(slabs))
        pairs.extend((s, c) for s in run)
    return pairs


def exchange(value, slabs, groups):
    order = [[c * slabs + s for s, c in chain(slabs, groups)]]
    return lax.all_to_all(value, AXES, 0, 0, tiled=True, axis_index_groups=order)


def unfold(value):
    groups = value.shape[0]
    return jnp.stack([value[c] if c % 2 == 0 else jnp.flip(value[c], 0) for c in range(groups)])


def neighbours(low, high, slabs, groups):
    devices = slabs * groups
    columns = low.shape[0]
    place = [s * groups + c for s, c in chain(slabs, groups)]
    left, right, found, hop = [], [], 0, 1
    while found < 3:
        count = min(columns, 3 - found)
        up = [(place[i], place[i + hop]) for i in range(devices - hop)]
        down = [(j, i) for i, j in up]
        left.insert(0, lax.ppermute(high[columns - count :], ("slab", "coil"), up))
        right.append(lax.ppermute(low[:count], ("slab", "coil"), down))
        found += count
        hop += 1
    return jnp.concatenate(left, axis=0), jnp.concatenate(right, axis=0)


def shards(image, sensitivity, kspace, sampled, w_in, w_mid, w_out):
    slabs, groups = lax.axis_size("slab"), lax.axis_size("coil")
    devices = slabs * groups
    _, local_z, ny, nx = image.shape
    local_coils = sensitivity.shape[1]
    coils = local_coils * groups
    nz, local_ky = kspace.shape[2:4]
    columns = nx // devices
    local_y = ny // groups

    map_slabs = 1 if local_z % 8 > 0 or local_coils > 1 else slabs
    data_slabs = 1 if local_ky % 8 > 0 or local_coils > 1 else slabs

    f32 = jnp.float32
    parts = math.gcd(local_z, groups)
    share = local_z // parts
    own = lax.dynamic_slice_in_dim(image, lax.axis_index("coil") % parts * share, share, 1)
    sent = [v.reshape(-1, ny, nx).astype(wire) for v in (sensitivity, own)]
    sent = lax.optimization_barrier(jnp.concatenate(sent, axis=0))
    sent = exchange(sent.transpose(2, 0, 1), slabs, groups)

    rows = rounded(2 * columns, 8)
    halo_rows = rounded(rows + 12, 16) - rows
    block = (columns + 2) // math.gcd(columns + 2, 2)
    weights = matrices(w_in, w_mid, w_out, columns, block, rows, halo_rows)
    slab, group = lax.axis_index("slab"), lax.axis_index("coil")
    chunk = group * slabs + jnp.where(group % 2 == 0, slab, slabs - 1 - slab)
    place = jnp.stack([chunk * columns, jnp.int32(nx)])
    re_x, im_x = (jnp.asarray(v, f32) for v in dft(nx))
    re_x, im_x = lax.optimization_barrier((re_x, im_x))
    transform_x = jnp.stack([re_x, im_x, -im_x, re_x]).reshape(2, 2, nx, nx)
    data = jnp.einsum("aczyr,baxr->xcbyz", kspace, transform_x, precision=three_pass)
    measured = sampled.T[None, None, None] > 0
    if data_slabs > 1:
        code = scale_code(jnp.max(jnp.abs(data), axis=(2, 4), keepdims=True))
        data = jnp.round(data * (0.5 / scale_of(code))).astype(jnp.int32)
        data = jnp.where(measured, data, -16384)
        data = (2 * data + low_bits(code, data.shape, 4)).astype(jnp.int16)
    else:
        data = jnp.where(measured, data, not_sampled).astype(wire)
    data = row_major(data)
    weights = [row_major(w) for w in weights]
    sent, data, weights, place = lax.optimization_barrier((sent, data, weights, place))

    data = exchange(data, slabs, groups)
    cut = 2 * local_coils * local_z
    maps = sent[:, :cut].reshape(groups, slabs, columns, 2, local_coils, local_z, ny)
    if map_slabs == 1:
        maps = unfold(maps)
    maps = maps.transpose(2, 0, 4, 3, 1, 5, 6).reshape(columns, coils, 2, nz, ny).astype(f32)
    own = unfold(sent[:, cut:].reshape(groups, slabs, columns, 2, share, ny)[:parts])
    own = own.transpose(2, 3, 1, 0, 4, 5).reshape(columns, 2, nz, ny).astype(f32)
    constants = transforms(nz, ny)
    first = first_spectrum(maps, own, constants, map_slabs)
    data, first = lax.optimization_barrier((data, first))
    if data_slabs == 1:
        data = unfold(data.reshape(groups, slabs, columns, local_coils, 2, local_ky, nz))
        data = data.transpose(2, 0, 3, 4, 1, 5, 6).reshape(columns, coils, 2, ny, nz)
    else:
        data = data.reshape(devices, columns, 2, local_ky, nz)
    current, low, high, misfit = gradient_steps(
        maps, own, first, data if data_slabs > 1 else data.astype(f32), constants, rows, slabs, map_slabs, data_slabs
    )
    if rows > 2 * columns:
        used = jnp.arange(rows, dtype=jnp.int32)[:, None] < 2 * columns
        current = jnp.where(used, current.reshape(nz, rows, ny), 0.0).reshape(-1, ny)

    received = neighbours(low, high, slabs, groups)
    if data_slabs == 1:
        misfit = misfit.astype(wire)
    misfit = misfit.reshape(groups, local_coils, slabs, columns, 2, local_ky, nz)
    misfit = misfit.transpose(0, 2, 3, 1, 4, 5, 6)
    if data_slabs == 1:
        misfit = unfold(misfit)
    misfit = misfit.reshape(devices, columns, local_coils, 2, local_ky, nz)
    received, misfit = lax.optimization_barrier((received, misfit))
    misfit = exchange(misfit, slabs, groups)

    aligned = columns == 8 and local_z % 2 == 0 and ny == 128 and groups == 2
    if aligned:
        shape = (groups, slabs, local_z * columns, ny)
        out_shape = jax.ShapeDtypeStruct(shape, jnp.int16)
    else:
        out_shape = jax.ShapeDtypeStruct((nz, rows, ny), f32)
    refined = denoise(place, current, *received, weights, out_shape)
    refined, misfit = lax.optimization_barrier((refined, misfit))

    misfit = misfit.reshape(nx, local_coils, 2, local_ky, nz)
    if data_slabs > 1:
        misfit = misfit.astype(jnp.int32)
        scale = scale_of(read_code(misfit[:, :, :1]))
    else:
        scale = 1.0 / wire_scale
    misfit = misfit.astype(f32) * scale
    residual = jnp.einsum("xcayz,abxr->bczyr", misfit, transform_x, precision=three_pass)

    if aligned:
        sent = refined.reshape(devices, -1, ny)
        sent = exchange(sent, slabs, groups)
        return unpack(sent, columns, local_z), residual
    refined = refined[:, : 2 * columns].reshape(nz, 2, columns, ny)
    largest = jnp.maximum(jnp.max(jnp.abs(refined)), 1e-30)
    exponent = jnp.ceil(jnp.log2(largest)) - 15.0
    sent = (refined * jnp.exp2(-exponent)).astype(wire)
    sent = sent.reshape(slabs, local_z, 2, columns, groups, local_y)
    sent = unfold(sent.transpose(4, 0, 3, 2, 1, 5))
    sent = sent.reshape(devices, columns, 2 * local_z * local_y)
    tag = jnp.broadcast_to(exponent.astype(wire), (devices, columns, ny))
    sent = jnp.concatenate([sent, tag], axis=2)
    sent = exchange(sent, slabs, groups)
    scale = jnp.exp2(sent[:, :, -1].astype(f32)).reshape(nx)
    refined = sent[:, :, :-ny].reshape(nx, 2, local_z, local_y).astype(f32)
    refined = refined.transpose(1, 2, 3, 0) * scale
    return (refined, residual)


def solution(mesh):
    placed = (
        P(None, "slab", None, None),
        P(None, "coil", "slab", None, None),
        P(None, "coil", None, "slab", None),
        P(None, "slab"),
        P(),
        P(),
        P(),
    )
    return jax.shard_map(
        shards,
        mesh=mesh,
        in_specs=placed,
        out_specs=(P(None, "slab", "coil", None), P(None, "coil", None, "slab", None)),
        check_vma=False,
    )
```

```python
import functools
import math

import jax
import jax.numpy as jnp
import numpy as np
from jax import lax
from jax.experimental import pallas as pl
from jax.experimental.layout import Layout, with_layout_constraint
from jax.experimental.pallas import tpu as pltpu
from jax.sharding import PartitionSpec as P

AXES = ("coil", "slab")
step_size = 0.5
three_pass = lax.Precision.HIGH
wire = jnp.float16
wire_scale = 2.0**-6
not_sampled = 60000.0
sampled_below = 30000.0
steps_per_octave = 64.0
code_bias = 8192.0


def dft(length):
    index = np.arange(length)
    angles = (index[:, None] * index[None, :] % length) * (2.0 * math.pi / length)
    factor = 1.0 / math.sqrt(length)
    return np.cos(angles) * factor, -np.sin(angles) * factor


def split_constant(value):
    value = jnp.asarray(value, jnp.float32)
    high = value.astype(jnp.bfloat16)
    return high, (value - high.astype(jnp.float32)).astype(jnp.bfloat16)


def complex_matrix(length):
    re, im = dft(length)
    return np.block([[re, im], [-im, re]])


def split(value):
    high = value.astype(jnp.bfloat16)
    low = (value - high.astype(jnp.float32)).astype(jnp.bfloat16)
    return high, low


def dot(a, b):
    return jnp.dot(a, b, preferred_element_type=jnp.float32)


def from_right(value, matrix):
    high, low = split(value)
    factor = jnp.concatenate([matrix[0], matrix[0], matrix[1]], axis=0)
    return dot(jnp.concatenate([high, low, high], axis=1), factor)


def from_left(matrix, value):
    high, low = split(value)
    factor = jnp.concatenate([matrix[0], matrix[0], matrix[1]], axis=1)
    return dot(factor, jnp.concatenate([high, low, high], axis=0))


def load(ref, *index):
    return ref[index].astype(jnp.float32)


def load_plane(ref, slabs, *index):
    plane = load(ref, *index)
    block = plane.shape[0] // slabs
    if slabs > 1 and index[1] % 2 == 1:
        parts = [plane[s * block : (s + 1) * block] for s in reversed(range(slabs))]
        plane = jnp.concatenate(parts, axis=0)
    return plane


def load_lines(ref, slabs, x, c):
    if slabs == 1:
        re, im = load(ref, x, c, 0), load(ref, x, c, 1)
        return re, im, jnp.where(re < sampled_below, 1.0, 0.0)
    senders = list(range(slabs)) if c % 2 == 0 else list(reversed(range(slabs)))

    def plane(k):
        blocks = [ref[c * slabs + s, x, k].astype(jnp.int32) for s in senders]
        return jnp.concatenate(blocks, axis=0)

    re, im = plane(0), plane(1)
    scale = scale_of(read_code(re))
    keep = jnp.where(re > -32766, 1.0, 0.0)
    return re.astype(jnp.float32) * scale, im.astype(jnp.float32) * scale, keep


def scale_code(largest):
    top = jnp.maximum(largest, 1e-30) * (1.0 / 32000.0)
    return jnp.ceil(jnp.log(top) * (steps_per_octave / math.log(2.0)))


def scale_of(code):
    return jnp.exp(code * (math.log(2.0) / steps_per_octave))


def low_bits(code, shape, axis):
    bias = jnp.broadcast_to((code + code_bias).astype(jnp.int32), shape)
    return (bias >> (lax.broadcasted_iota(jnp.int32, shape, axis) & 15)) & 1


def read_code(value):
    lane = lax.broadcasted_iota(jnp.int32, value.shape, value.ndim - 1)
    bits = jnp.where(lane < 16, (value & 1) << (lane & 15), 0).astype(jnp.float32)
    return jnp.sum(bits, axis=-1, keepdims=True) - code_bias


def to_spectrum(maps, slabs, x, estimate, y_right, z_left):
    coils, _, nz, ny = maps.shape[1:]
    cur_re, cur_im = estimate
    pieces = []
    for c in range(coils):
        map_re, map_im = (load_plane(maps, slabs, x, c, k) for k in range(2))
        coil_re = map_re * cur_re - map_im * cur_im
        coil_im = map_re * cur_im + map_im * cur_re
        pieces.append(jnp.concatenate([coil_re, coil_im], axis=1))
    over_y = from_right(jnp.concatenate(pieces, axis=0), y_right)
    planes = [over_y[c * nz : (c + 1) * nz] for c in range(coils)]
    upper = jnp.concatenate([p[:, :ny] for p in planes], axis=1)
    lower = jnp.concatenate([p[:, ny:] for p in planes], axis=1)
    return from_left(z_left, jnp.concatenate([upper, lower], axis=0))


def to_gradient(maps, slabs, x, misfit, y_back, z_back):
    coils, _, nz, ny = maps.shape[1:]
    over_z = from_left(z_back, misfit)
    pieces = []
    for c in range(coils):
        lanes = slice(c * ny, (c + 1) * ny)
        pieces.append(jnp.concatenate([over_z[:nz, lanes], over_z[nz:, lanes]], axis=1))
    back = from_right(jnp.concatenate(pieces, axis=0), y_back)
    grad_re = jnp.zeros((nz, ny), jnp.float32)
    grad_im = jnp.zeros((nz, ny), jnp.float32)
    for c in range(coils):
        map_re, map_im = (load_plane(maps, slabs, x, c, k) for k in range(2))
        back_re = back[c * nz : (c + 1) * nz, :ny]
        back_im = back[c * nz : (c + 1) * nz, ny:]
        grad_re += map_re * back_re + map_im * back_im
        grad_im += map_re * back_im - map_im * back_re
    return grad_re, grad_im


def spectrum_kernel(slabs, maps, image, y_right, z_left, spectrum):
    for x in range(maps.shape[0]):
        estimate = (load(image, x, 0), load(image, x, 1))
        spectrum[x] = to_spectrum(maps, slabs, x, estimate, y_right, z_left)


def gradient_kernel(slabs, data_slabs, maps, image, first, data, y_right, y_back, z_left, z_back, current, low, high, residual):
    columns, coils, _, nz, ny = maps.shape
    step = pl.program_id(0)
    total = columns * pl.num_programs(0)
    rows = current.shape[0] // nz
    edge = low.shape[0]

    measured, masks, estimates = [], [], []
    for x in range(columns):
        lines = [[v.T for v in load_lines(data, data_slabs, x, c)] for c in range(coils)]
        data_re, data_im, keep = (jnp.concatenate(v, axis=1) for v in zip(*lines))
        measured.append(jnp.concatenate([data_re, data_im], axis=0))
        masks.append(jnp.concatenate([keep, keep], axis=0))
        estimates.append((load(image, x, 0), load(image, x, 1)))
    spectra = [first[x] for x in range(columns)]
    misfits = None
    for repeat in range(2):
        if repeat > 0:
            spectra = [
                to_spectrum(maps, slabs, x, estimates[x], y_right, z_left) for x in range(columns)
            ]
        misfits = [masks[x] * (spectra[x] - measured[x]) for x in range(columns)]
        gradients = [to_gradient(maps, slabs, x, misfits[x], y_back, z_back) for x in range(columns)]
        estimates = [
            tuple(e - step_size * g for e, g in zip(estimates[x], gradients[x]))
            for x in range(columns)
        ]
    for x in range(columns):
        column = step * columns + x
        rounded_parts = [part.astype(jnp.bfloat16) for part in estimates[x]]
        for k in range(2):
            current[pl.ds(k * total + column, nz, stride=rows), :] = estimates[x][k]

        @pl.when(column < edge)
        def _():
            for k in range(2):
                low[column, k] = rounded_parts[k]

        @pl.when(column >= total - edge)
        def _():
            for k in range(2):
                high[column - (total - edge), k] = rounded_parts[k]

        for c in range(coils):
            lanes = slice(c * ny, (c + 1) * ny)
            planes = [misfits[x][k * nz : (k + 1) * nz, lanes].T for k in range(2)]
            if data_slabs == 1:
                for k in range(2):
                    residual[x, c, k] = planes[k] * wire_scale
                continue
            largest = jnp.maximum(jnp.abs(planes[0]), jnp.abs(planes[1]))
            code = scale_code(jnp.max(largest, axis=1, keepdims=True))
            half = 0.5 / scale_of(code)
            bits = low_bits(code, (ny, nz), 1)
            local_ky = ny // data_slabs
            for k in range(2):
                plane = 2 * jnp.round(planes[k] * half).astype(jnp.int32) + bits
                plane = plane.astype(jnp.int16)
                for i in range(data_slabs):
                    to = i if c % 2 == 0 else data_slabs - 1 - i
                    residual[c, to, x, k] = plane[i * local_ky : (i + 1) * local_ky]


def column_spec(shape, together):
    return pl.BlockSpec((together,) + shape[1:], lambda i: (i,) + (0,) * (len(shape) - 1))


def fixed_spec(shape):
    return pl.BlockSpec(shape, lambda i: (0,) * len(shape))


def transforms(nz, ny):
    right = {n: jnp.stack(split_constant(complex_matrix(n))) for n in {ny, nz}}
    left = {n: jnp.stack(split_constant(complex_matrix(n).T)) for n in {ny, nz}}
    return right[ny], left[ny], left[nz], right[nz]


def first_spectrum(maps, image, constants, slabs):
    columns, coils, _, nz, ny = maps.shape
    together = math.gcd(columns, 2)
    used = [constants[0], constants[2]]
    shape = (columns, 2 * nz, coils * ny)
    return pl.pallas_call(
        functools.partial(spectrum_kernel, slabs),
        grid=(columns // together,),
        in_specs=[column_spec(maps.shape, together), column_spec(image.shape, together)]
        + [fixed_spec(c.shape) for c in used],
        out_specs=column_spec(shape, together),
        out_shape=jax.ShapeDtypeStruct(shape, jnp.float32),
        name="first_spectrum",
    )(maps, image, *used)


def gradient_steps(maps, image, first, data, constants, rows, slabs, map_slabs, data_slabs):
    columns, coils, _, nz, ny = maps.shape
    together = math.gcd(columns, 2)
    edge = min(3, columns)
    edges = (edge, 2, nz, ny)
    local_ky = ny // slabs
    if data_slabs > 1:
        shape = (coils, slabs, columns, 2, local_ky, nz)
        block = (coils, slabs, together, 2, local_ky, nz)
        residual_spec = pl.BlockSpec(block, lambda i: (0, 0, i, 0, 0, 0))
        block = (coils * slabs, together, 2, local_ky, nz)
        data_spec = pl.BlockSpec(block, lambda i: (0, i, 0, 0, 0))
    else:
        shape = data.shape
        residual_spec = data_spec = column_spec(shape, together)
    current, low, high, misfit = pl.pallas_call(
        functools.partial(gradient_kernel, map_slabs, data_slabs),
        grid=(columns // together,),
        in_specs=[column_spec(v.shape, together) for v in (maps, image, first)]
        + [data_spec]
        + [fixed_spec(c.shape) for c in constants],
        out_specs=[
            fixed_spec((nz * rows, ny)),
            fixed_spec(edges),
            fixed_spec(edges),
            residual_spec,
        ],
        out_shape=[
            jax.ShapeDtypeStruct((nz * rows, ny), jnp.float32),
            jax.ShapeDtypeStruct(edges, jnp.bfloat16),
            jax.ShapeDtypeStruct(edges, jnp.bfloat16),
            jax.ShapeDtypeStruct(shape, jnp.int16 if data_slabs > 1 else jnp.float32),
        ],
        name="gradient_steps",
    )(maps, image, first, data, *constants)
    if misfit.ndim == 5:
        misfit = misfit.reshape(columns, coils, 2, slabs, local_ky, nz).transpose(1, 3, 0, 2, 4, 5)
    return current, low, high, misfit


def row_major(value):
    return with_layout_constraint(value, Layout(major_to_minor=tuple(range(value.ndim))))


def rounded(count, unit):
    return -(-count // unit) * unit


def banded(weight, columns_out, order):
    columns_in = columns_out + 2
    select = np.zeros((3, columns_out, columns_in), np.float32)
    for shift in range(3):
        select[shift, np.arange(columns_out), np.arange(columns_out) + shift] = 1.0
    taps = weight.reshape((3, 3, 3) + weight.shape[1:])
    return jnp.einsum("zyxoj,xab->" + order, taps, jnp.asarray(select, weight.dtype))


def matrices(w_in, w_mid, w_out, columns, block, rows, halo_rows):
    feat = w_mid.shape[1]
    first = banded(w_in, columns + 4, "aozyjb")
    own = first[..., 3 : columns + 3].reshape(-1, 3, 3, 2 * columns)
    own = jnp.pad(own, ((0, 0),) * 3 + ((0, rows - 2 * columns),))
    sides = jnp.concatenate([first[..., :3], first[..., columns + 3 :]], axis=-1)
    sides = jnp.swapaxes(sides, -1, -2).reshape(-1, 3, 3, 12)
    sides = jnp.pad(sides, ((0, 0),) * 3 + ((0, halo_rows - 12),))
    first = jnp.concatenate([own, sides], axis=-1).reshape((columns + 4) * feat, -1)
    middle = banded(w_mid, block, "yaozbj").reshape(3 * block * feat, -1)
    last = banded(w_out, columns, "zyoabj").reshape(9, 2 * columns, -1)
    last = jnp.pad(last, ((0, 0), (0, rows - 2 * columns), (0, 0)))
    return first, middle, last.reshape(9 * rows, -1)


def conv_kernel(place, current, left, right, w_in, w_mid, w_out, packed, pad_0, pad_1, pad_2, halo, refined):
    rows_1, rows_2 = pad_1.shape[1], pad_2.shape[1]
    nz, ny = refined.shape[0], refined.shape[2]
    rows = refined.shape[1]
    halo_rows = halo.shape[0] // nz
    bf16, f32 = jnp.bfloat16, jnp.float32

    for ref in (pad_0, pad_1):
        empty = jnp.zeros(ref.shape[1:], ref.dtype)
        ref[0] = empty
        ref[nz + 1] = empty

    def shifted(value, by):
        lane = lax.broadcasted_iota(jnp.int32, value.shape, 1)
        edge = 0 if by == 1 else ny - 1
        return jnp.where(lane == edge, 0.0, pltpu.roll(value, by % ny, 1))

    def inside(count, before):
        feat = (rows_1 - rows_2) // 2
        row = lax.broadcasted_iota(jnp.int32, (count, ny), 0)
        x = place[0] - before + row // feat
        return jnp.where((x >= 0) & (x < place[1]), 1.0, 0.0)

    keep_1, keep_2 = inside(rows_1, 2), inside(rows_2, 1)

    for side, ref in enumerate((left, right)):
        for column in range(3):
            for k in range(2):
                row = 6 * side + 2 * column + k
                halo[pl.ds(row, nz, stride=halo_rows), :] = ref[column, k].astype(f32)
    for row in range(12, halo_rows):
        halo[pl.ds(row, nz, stride=halo_rows), :] = jnp.zeros((nz, ny), f32)

    def spread(z, carry):
        own = current[pl.ds(pl.multiple_of(z * rows, 8), rows), :]
        sides = halo[pl.ds(pl.multiple_of(z * halo_rows, 8), halo_rows), :]
        value = jnp.concatenate([own, sides], axis=0)
        shifts = [shifted(value, 1), value, shifted(value, -1)]
        pad_0[z + 1] = jnp.concatenate(shifts, axis=0).astype(bf16)
        return carry

    def pair(block):
        near = jnp.concatenate([block[0], block[1], block[2]], axis=0)
        far = jnp.concatenate([block[1], block[2], block[3]], axis=0)
        return jnp.concatenate([near, far], axis=1)

    def first(i):
        out = dot(w_in[...], pair(pad_0[pl.ds(2 * i, 4)]))
        for k in range(2):
            part = jnp.maximum(out[:, k * ny : (k + 1) * ny], 0.0) * keep_1
            pad_1[2 * i + k + 1] = part.astype(bf16)

    block_out = w_mid.shape[0] // 3
    block_in = w_mid.shape[1] // 3

    def middle(i):
        for b in range(rows_2 // block_out):
            low = b * block_out
            out = dot(w_mid[...], pair(pad_1[pl.ds(2 * i, 4), low : low + block_in]))
            for k in range(2):
                part = out[:, k * ny : (k + 1) * ny]
                total = part[block_out : 2 * block_out]
                total = total + shifted(part[:block_out], 1)
                total = total + shifted(part[2 * block_out :], -1)
                total = jnp.maximum(total, 0.0) * keep_2[low : low + block_out]
                pad_2[2 * i + k, low : low + block_out] = total.astype(bf16)

    def finish(z, total, largest):
        out = total[rows : 2 * rows]
        out = out + shifted(total[:rows], 1) + shifted(total[2 * rows :], -1)
        out = out + current[pl.ds(pl.multiple_of(z * rows, 8), rows), :]
        refined[z] = out
        return jnp.maximum(largest, jnp.abs(out))

    def last(i, carry):
        older, newer, largest = carry
        both = jnp.concatenate([pad_2[2 * i], pad_2[2 * i + 1]], axis=1)
        out = dot(w_out[...], both)
        for k in range(2):
            part = out[:, k * ny : (k + 1) * ny]
            z = 2 * i + k - 1
            total = older + part[6 * rows :]
            if k == 0:
                total = jnp.where(i > 0, total, 0.0)
            largest = finish(jnp.maximum(z, 0), total, largest)
            older, newer = newer + part[3 * rows : 6 * rows], part[: 3 * rows]
        return older, newer, largest

    lax.fori_loop(0, nz, spread, 0, unroll=4)

    def alone(step):
        def run(i, carry):
            step(i)
            return carry

        return run

    lax.fori_loop(0, nz // 2, alone(first), 0, unroll=8)
    lax.fori_loop(0, nz // 2, alone(middle), 0, unroll=8)
    sums = jnp.zeros((3 * rows, ny), f32)
    carry = (sums, sums, jnp.zeros((rows, ny), f32))
    older, _, largest = lax.fori_loop(0, nz // 2, last, carry, unroll=8)
    largest = finish(nz - 1, older, largest)

    if packed.dtype != jnp.int16:
        packed[...] = refined[...]
        return

    _, slabs = packed.shape[:2]
    columns = rows // 2
    code = scale_code(jnp.max(largest, axis=(0, 1), keepdims=True))
    factor = 1.0 / scale_of(code)
    lane = lax.broadcasted_iota(jnp.int32, (columns, ny), 1)
    bits = low_bits(code, (16, ny), 0)

    def pack(s, carry):
        for z in range(0, nz // slabs, 2):
            halves = [[], []]
            for k in range(2):
                value = refined[s * (nz // slabs) + z + k] * (factor * (0.5 if z == 0 else 1.0))
                value = jnp.round(value)
                re, im = value[:columns], value[columns:]
                halves[0].append(jnp.where(lane < ny // 2, re, pltpu.roll(im, ny // 2, 1)))
                halves[1].append(jnp.where(lane < ny // 2, pltpu.roll(re, ny // 2, 1), im))
            for c in range(2):
                both = jnp.concatenate(halves[c], axis=0).astype(jnp.int32)
                if z == 0:
                    both = 2 * both + bits
                to = s if c == 0 else slabs - 1 - s
                packed[c, to, z * columns : (z + 2) * columns] = both.astype(jnp.int16)
        return carry

    lax.fori_loop(0, slabs, pack, 0)


def denoise(place, current, left, right, weights, out_shape):
    w_in, w_mid, w_out = weights
    nz, ny = left.shape[2:]
    rows = current.shape[0] // nz
    halo_rows = w_in.shape[1] // 9 - rows
    flops = nz * ny * sum(2 * m.shape[0] * m.shape[1] for m in weights)
    return pl.pallas_call(
        conv_kernel,
        in_specs=[pl.BlockSpec(memory_space=pltpu.SMEM)]
        + [pl.BlockSpec(memory_space=pltpu.VMEM)] * 6,
        out_specs=pl.BlockSpec(memory_space=pltpu.VMEM),
        out_shape=out_shape,
        scratch_shapes=[
            pltpu.VMEM((nz + 2, w_in.shape[1] // 3, ny), jnp.bfloat16),
            pltpu.VMEM((nz + 2, w_in.shape[0], ny), jnp.bfloat16),
            pltpu.VMEM((nz, w_out.shape[1], ny), jnp.bfloat16),
            pltpu.VMEM((nz * halo_rows, ny), jnp.float32),
            pltpu.VMEM((nz, rows, ny), jnp.float32),
        ],
        cost_estimate=pl.CostEstimate(
            flops=flops, transcendentals=0, bytes_accessed=8 * current.size
        ),
        name="denoise",
    )(place, current, left, right, w_in, w_mid, w_out)


def unpack_kernel(values, tag, out):
    devices, both, lanes = values.shape
    columns = both // 2
    bits = tag[...].astype(jnp.int32) & 1
    bits = bits << lax.broadcasted_iota(jnp.int32, bits.shape, 1)
    code = jnp.sum(bits.astype(jnp.float32), axis=1, keepdims=True) - code_bias
    factor = scale_of(code)
    value = values[...].astype(jnp.int32).astype(jnp.float32) * factor
    for k in range(2):
        plane = value[:, k * columns : (k + 1) * columns].reshape(devices * columns, lanes)
        plane = plane.T
        out[0, k] = plane[: lanes // 2]
        out[1, k] = plane[lanes // 2 :]


def unpack(sent, columns, local_z):
    devices, _, lanes = sent.shape
    some = devices
    return pl.pallas_call(
        unpack_kernel,
        grid=(local_z // 2, devices // some),
        in_specs=[
            pl.BlockSpec((some, 2 * columns, lanes), lambda i, j: (j, i, 0)),
            pl.BlockSpec((some, 16, lanes), lambda i, j: (j, 0, 0)),
        ],
        out_specs=pl.BlockSpec((2, 2, lanes // 2, some * columns), lambda i, j: (0, i, 0, j)),
        out_shape=jax.ShapeDtypeStruct(
            (2, local_z, lanes // 2, devices * columns), jnp.float32
        ),
        name="unpack",
    )(sent, sent)


def chain(slabs, groups):
    pairs = []
    for c in range(groups):
        run = range(slabs) if c % 2 == 0 else reversed(range(slabs))
        pairs.extend((s, c) for s in run)
    return pairs


def exchange(value, slabs, groups):
    order = [[c * slabs + s for s, c in chain(slabs, groups)]]
    return lax.all_to_all(value, AXES, 0, 0, tiled=True, axis_index_groups=order)


def unfold(value):
    groups = value.shape[0]
    return jnp.stack([value[c] if c % 2 == 0 else jnp.flip(value[c], 0) for c in range(groups)])


def neighbours(low, high, slabs, groups):
    devices = slabs * groups
    columns = low.shape[0]
    place = [s * groups + c for s, c in chain(slabs, groups)]
    left, right, found, hop = [], [], 0, 1
    while found < 3:
        count = min(columns, 3 - found)
        up = [(place[i], place[i + hop]) for i in range(devices - hop)]
        down = [(j, i) for i, j in up]
        left.insert(0, lax.ppermute(high[columns - count :], ("slab", "coil"), up))
        right.append(lax.ppermute(low[:count], ("slab", "coil"), down))
        found += count
        hop += 1
    return jnp.concatenate(left, axis=0), jnp.concatenate(right, axis=0)


def shards(image, sensitivity, kspace, sampled, w_in, w_mid, w_out):
    slabs, groups = lax.axis_size("slab"), lax.axis_size("coil")
    devices = slabs * groups
    _, local_z, ny, nx = image.shape
    local_coils = sensitivity.shape[1]
    coils = local_coils * groups
    nz, local_ky = kspace.shape[2:4]
    columns = nx // devices
    local_y = ny // groups

    map_slabs = 1 if local_z % 8 > 0 or local_coils > 1 else slabs
    data_slabs = 1 if local_ky % 8 > 0 or local_coils > 1 else slabs

    f32 = jnp.float32
    parts = math.gcd(local_z, groups)
    share = local_z // parts
    own = lax.dynamic_slice_in_dim(image, lax.axis_index("coil") % parts * share, share, 1)
    sent = [v.reshape(-1, ny, nx).astype(wire) for v in (sensitivity, own)]
    sent = lax.optimization_barrier(jnp.concatenate(sent, axis=0))
    sent = exchange(sent.transpose(2, 0, 1), slabs, groups)

    rows = rounded(2 * columns, 8)
    halo_rows = rounded(rows + 12, 16) - rows
    block = (columns + 2) // math.gcd(columns + 2, 2)
    weights = matrices(w_in, w_mid, w_out, columns, block, rows, halo_rows)
    slab, group = lax.axis_index("slab"), lax.axis_index("coil")
    chunk = group * slabs + jnp.where(group % 2 == 0, slab, slabs - 1 - slab)
    place = jnp.stack([chunk * columns, jnp.int32(nx)])
    re_x, im_x = (jnp.asarray(v, f32) for v in dft(nx))
    re_x, im_x = lax.optimization_barrier((re_x, im_x))
    transform_x = jnp.stack([re_x, im_x, -im_x, re_x]).reshape(2, 2, nx, nx)
    data = jnp.einsum("aczyr,baxr->xcbyz", kspace, transform_x, precision=three_pass)
    measured = sampled.T[None, None, None] > 0
    if data_slabs > 1:
        code = scale_code(jnp.max(jnp.abs(data), axis=(2, 4), keepdims=True))
        data = jnp.round(data * (0.5 / scale_of(code))).astype(jnp.int32)
        data = jnp.where(measured, data, -16384)
        data = (2 * data + low_bits(code, data.shape, 4)).astype(jnp.int16)
    else:
        data = jnp.where(measured, data, not_sampled).astype(wire)
    data = row_major(data)
    weights = [row_major(w) for w in weights]
    sent, data, weights, place = lax.optimization_barrier((sent, data, weights, place))

    data = exchange(data, slabs, groups)
    cut = 2 * local_coils * local_z
    maps = sent[:, :cut].reshape(groups, slabs, columns, 2, local_coils, local_z, ny)
    if map_slabs == 1:
        maps = unfold(maps)
    maps = maps.transpose(2, 0, 4, 3, 1, 5, 6).reshape(columns, coils, 2, nz, ny).astype(f32)
    own = unfold(sent[:, cut:].reshape(groups, slabs, columns, 2, share, ny)[:parts])
    own = own.transpose(2, 3, 1, 0, 4, 5).reshape(columns, 2, nz, ny).astype(f32)
    constants = transforms(nz, ny)
    first = first_spectrum(maps, own, constants, map_slabs)
    data, first = lax.optimization_barrier((data, first))
    if data_slabs == 1:
        data = unfold(data.reshape(groups, slabs, columns, local_coils, 2, local_ky, nz))
        data = data.transpose(2, 0, 3, 4, 1, 5, 6).reshape(columns, coils, 2, ny, nz)
    else:
        data = data.reshape(devices, columns, 2, local_ky, nz)
    current, low, high, misfit = gradient_steps(
        maps, own, first, data if data_slabs > 1 else data.astype(f32), constants, rows, slabs, map_slabs, data_slabs
    )
    if rows > 2 * columns:
        used = jnp.arange(rows, dtype=jnp.int32)[:, None] < 2 * columns
        current = jnp.where(used, current.reshape(nz, rows, ny), 0.0).reshape(-1, ny)

    received = neighbours(low, high, slabs, groups)
    if data_slabs == 1:
        misfit = misfit.astype(wire)
    misfit = misfit.reshape(groups, local_coils, slabs, columns, 2, local_ky, nz)
    misfit = misfit.transpose(0, 2, 3, 1, 4, 5, 6)
    if data_slabs == 1:
        misfit = unfold(misfit)
    misfit = misfit.reshape(devices, columns, local_coils, 2, local_ky, nz)
    misfit = exchange(misfit, slabs, groups)

    aligned = columns == 8 and local_z % 2 == 0 and ny == 128 and groups == 2
    if aligned:
        shape = (groups, slabs, local_z * columns, ny)
        out_shape = jax.ShapeDtypeStruct(shape, jnp.int16)
    else:
        out_shape = jax.ShapeDtypeStruct((nz, rows, ny), f32)
    refined = denoise(place, current, *received, weights, out_shape)
    refined, misfit = lax.optimization_barrier((refined, misfit))

    misfit = misfit.reshape(nx, local_coils, 2, local_ky, nz)
    if data_slabs > 1:
        misfit = misfit.astype(jnp.int32)
        scale = scale_of(read_code(misfit[:, :, :1]))
    else:
        scale = 1.0 / wire_scale
    misfit = misfit.astype(f32) * scale
    residual = jnp.einsum("xcayz,abxr->bczyr", misfit, transform_x, precision=three_pass)

    if aligned:
        sent = refined.reshape(devices, -1, ny)
        sent = exchange(sent, slabs, groups)
        return unpack(sent, columns, local_z), residual
    refined = refined[:, : 2 * columns].reshape(nz, 2, columns, ny)
    largest = jnp.maximum(jnp.max(jnp.abs(refined)), 1e-30)
    exponent = jnp.ceil(jnp.log2(largest)) - 15.0
    sent = (refined * jnp.exp2(-exponent)).astype(wire)
    sent = sent.reshape(slabs, local_z, 2, columns, groups, local_y)
    sent = unfold(sent.transpose(4, 0, 3, 2, 1, 5))
    sent = sent.reshape(devices, columns, 2 * local_z * local_y)
    tag = jnp.broadcast_to(exponent.astype(wire), (devices, columns, ny))
    sent = jnp.concatenate([sent, tag], axis=2)
    sent = exchange(sent, slabs, groups)
    scale = jnp.exp2(sent[:, :, -1].astype(f32)).reshape(nx)
    refined = sent[:, :, :-ny].reshape(nx, 2, local_z, local_y).astype(f32)
    refined = refined.transpose(1, 2, 3, 0) * scale
    return (refined, residual)


def solution(mesh):
    placed = (
        P(None, "slab", None, None),
        P(None, "coil", "slab", None, None),
        P(None, "coil", None, "slab", None),
        P(None, "slab"),
        P(),
        P(),
        P(),
    )
    return jax.shard_map(
        shards,
        mesh=mesh,
        in_specs=placed,
        out_specs=(P(None, "slab", "coil", None), P(None, "coil", None, "slab", None)),
        check_vma=False,
    )
```
